32 devices in a mesh: tile: 16 (over z, x, core), rep: 2 (over y).
Axes of the slice: x: 2, y: 2, z: 4, core: 2. Of those that a mesh axis runs over, the one named last changes fastest.
Arguments:
- waves: bfloat16 [2, 8192, 128], P('rep', 'tile'), may hold values from -6 to 6
- dest_tile: int32 [2, 8192, 1], P('rep', 'tile'), may hold values from 0 to 15; in each aligned block of 512 rows (0 to 511, 512 to 1023, ..., all dimensions but the last counted through in order) at most 32 rows name the same one
- pixel_bin: int32 [2, 8192], P('rep', 'tile'), may hold values from 0 to 1023
- target: float32 [2, 128, 128], P('rep', 'tile'), may hold values from -6 to 6
- conv_one: bfloat16 [3, 3, 128, 128], replicated, may hold values from -0.1875 to 0.1875
- bias_one: float32 [128], replicated, may hold values from -0.5 to 0.5
- conv_two: bfloat16 [3, 3, 128], replicated, may hold values from -0.1875 to 0.1875
- bias_two: float32 [1], replicated, may hold values from -1 to 1
Outputs:
- prediction: float32 [2, 128, 128], P('rep', 'tile')
- update_one: float32 [3, 3, 128, 128], replicated
- update_bias: float32 [128], replicated
- update_two: float32 [3, 3, 128], replicated
The draws below stay inside these ranges and needn't reach their ends.
Inputs may be any that keep to these rules, and one draw needn't show every extreme that they name: `dest_tile`: among the rows of one device, no strip is named more than 32 times, a bound that some block reaches.
All inputs are finite; a program needn't handle non-finite values.
Results may differ from the reference program's by a relative error of at most 0.0024.
The reference program's roundings to bfloat16 on the way (of `grid`, `hidden`, `error` and `slope`) count: a program that leaves them out, or rounds other values in their place, can miss the bound.
Values may be sent and summed in bfloat16 or wider, within the bound.
A program may use at most 64 MiB of HBM per device.

```python
import math
import jax
import jax.numpy as jnp
import numpy as np
from jax import lax

STEPS = 128
C1 = 128
ROWS = 512
W = 128
CAP = 32
PIX = 1024
NH = 128
N_TILE = 16
N_REP = 2


def with_ends(drawn, rng, least, top_value):
    place = [jax.random.randint(jax.random.fold_in(rng, axis), (), 0, length) for axis, length in enumerate(drawn.shape)]
    longest = drawn.shape.index(max(drawn.shape))
    next_to = place[:longest] + [(place[longest] + 1) % drawn.shape[longest]] + place[longest + 1:]
    return drawn.at[tuple(place)].set(least).at[tuple(next_to)].set(top_value)


def block_scale(key, dims, pieces, low, largest):
    gain, own = 1.0, jax.random.fold_in(key, 6)
    for axis_at, blocks in pieces:
        draws = jnp.exp(jax.random.uniform(jax.random.fold_in(own, axis_at), (blocks,), jnp.float32, low / len(pieces), largest / len(pieces)))
        gain = gain * jnp.repeat(draws, dims[axis_at] // blocks).reshape([-1 if axis == axis_at else 1 for axis in range(len(dims))])
    return gain


def shared_out(rng, own, number, rows, amount, top, most, skew):
    sequence = jax.random.permutation(rng, amount)
    heavy_load, ordinary = shares(amount, rows * top, most, skew, True), shares(amount, rows * top, most, skew, False)
    places = jnp.arange(amount)

    def named(lengths, turn):
        used = int((lengths > 0).sum())
        fixed = max(1, used // 4)
        moved = fixed + (places - fixed + turn * (used - fixed)) % max(1, amount - fixed)
        return jnp.zeros((amount,), jnp.int32).at[sequence[jnp.where(places < fixed, places, moved)]].set(jnp.asarray(lengths, jnp.int32))

    lengths = jnp.where(number % 4 == 0, named(heavy_load, number // 4), named(ordinary, number - number // 4 - 1))
    mixed = jax.random.permutation(jax.random.fold_in(own, 3), amount)
    source_of, taker = mixed[0:amount // 2 * 2:2], mixed[1:amount // 2 * 2:2]
    slack = jnp.minimum(lengths[source_of] - 1, most - lengths[taker]) // 2
    slack = jnp.where((source_of == sequence[0]) | (taker == sequence[0]) | (lengths[taker] == 0), 0, jnp.maximum(slack, 0))
    moved = jax.random.randint(jax.random.fold_in(own, 4), (amount // 2,), 0, 1 << 20) % (slack + 1)
    lengths = lengths.at[source_of].add(-moved).at[taker].add(moved)
    members = jnp.searchsorted(jnp.cumsum(lengths), jnp.arange(rows * top), side="right").astype(jnp.int32)
    listing = members.reshape(top, rows).T
    listing = listing[jax.random.permutation(jax.random.fold_in(own, 1), rows)]
    turn = jax.random.randint(jax.random.fold_in(own, 2), (rows, 1), 0, top)
    return jnp.take_along_axis(listing, (jnp.arange(top)[None, :] + turn) % top, axis=1)


def shares(count, total, most, skew, full):
    portions = [(1 << 20) // math.isqrt(rank ** skew) + 1 for rank in range(1, count + 1)]
    largest = most if full else min(most, max(-(-total // count), total * portions[0] // sum(portions)))
    least = 1 if total - largest >= count - 1 else 0
    counts, surplus = [largest] + [least] * (count - 1), total - largest - least * (count - 1)
    while surplus > 0:
        candidates = [i for i in range(1, count) if counts[i] < largest] or [i for i in range(1, count) if counts[i] < most]
        mass, remaining = sum([portions[i] for i in candidates]), surplus
        for i in candidates:
            extra = min(most - counts[i], max(1, remaining * portions[i] // mass), surplus)
            counts[i] = counts[i] + extra
            surplus = surplus - extra
    return np.array(counts)


def scatter_about(key, shape, deviation, most, split=(), dtype=jnp.bfloat16):
    values = jax.random.normal(key, shape, jnp.float32) * deviation
    if len(split) > 0:
        values = block_scale(key, shape, split, -0.22, 0.18) * values
    return jnp.clip(values, min=-most, max=most).astype(dtype)


def setup_inputs(seed: int = 0) -> dict:
    key_list = jax.random.split(jax.random.key(seed), 9)
    waves = scatter_about(key_list[0], (N_REP, N_TILE * ROWS, STEPS), 1.0, 6.0, ((0, 2), (1, 16)))
    dest_tile_keys = jax.random.split(jax.random.fold_in(key_list[1], 1), N_REP * (N_TILE * ROWS) // ROWS)
    dest_tile_turns = jax.random.permutation(jax.random.fold_in(key_list[1], 3), N_REP * (N_TILE * ROWS) // ROWS)
    dest_tile = jax.vmap(lambda own, number: shared_out(jax.random.fold_in(key_list[1], 2), own, number, ROWS, N_TILE, 1, CAP, 2))(dest_tile_keys, dest_tile_turns).reshape((N_REP, N_TILE * ROWS, 1))
    pixel_bin = with_ends(jax.random.randint(key_list[2], (N_REP, N_TILE * ROWS), 0, PIX), jax.random.fold_in(key_list[2], 1), 0, PIX - 1).astype(jnp.int32)
    target = scatter_about(key_list[3], (N_REP, NH, W), 1.0, 6.0, ((0, 2), (1, 16)), jnp.float32)
    conv_one = scatter_about(key_list[4], (3, 3, STEPS, C1), (9 * STEPS) ** -0.5, 0.1875)
    bias_one = jnp.clip(jax.random.uniform(key_list[5], (C1,), jnp.float32, -0.5, 0.5), -0.5, 0.5)
    conv_two = scatter_about(key_list[6], (3, 3, C1), (9 * C1) ** -0.5, 0.1875)
    bias_two = jnp.clip(jax.random.uniform(key_list[7], (1,), jnp.float32, -1.0, 1.0), -1.0, 1.0)
    return {"waves": waves, "dest_tile": dest_tile, "pixel_bin": pixel_bin, "target": target, "conv_one": conv_one, "bias_one": bias_one, "conv_two": conv_two, "bias_two": bias_two}


def replica_terms(wave_rows, dest_rows, bin_rows, target_map, conv_one, bias_one, conv_two, bias_two):
    ids = dest_rows[:, 0] * PIX + bin_rows
    grid = jax.ops.segment_sum(wave_rows.astype(jnp.float32), ids, num_segments=N_TILE * PIX)
    grid = grid.astype(jnp.bfloat16).reshape(NH, W, STEPS)
    padded = jnp.pad(grid, ((2, 2), (2, 2), (0, 0)))
    pre = jnp.zeros((NH * W, C1), jnp.float32) + bias_one[None, :]
    for i in range(3):
        for j in range(3):
            patch = padded[2 * i:2 * i + NH, 2 * j:2 * j + W, :].reshape(NH * W, STEPS)
            pre = pre + jnp.dot(patch, conv_one[i, j], preferred_element_type=jnp.float32)
    pre = pre.reshape(NH, W, C1)
    hidden = jax.nn.silu(pre).astype(jnp.bfloat16)
    hidden_pad = jnp.pad(hidden, ((1, 1), (1, 1), (0, 0)))
    pred = jnp.zeros((NH, W), jnp.float32) + bias_two[0]
    for i in range(3):
        for j in range(3):
            pred = pred + jnp.einsum('hwc,c->hw', hidden_pad[i:i + NH, j:j + W, :].astype(jnp.float32), conv_two[i, j].astype(jnp.float32))
    error = ((pred - target_map) / N_REP).astype(jnp.bfloat16)
    error_pad = jnp.pad(error, ((1, 1), (1, 1)))
    grad_two = []
    back = jnp.zeros((NH, W, C1), jnp.float32)
    for i in range(3):
        for j in range(3):
            grad_two.append(jnp.einsum('hwc,hw->c', hidden_pad[i:i + NH, j:j + W, :].astype(jnp.float32), error.astype(jnp.float32)))
            shifted = error_pad[2 - i:2 - i + NH, 2 - j:2 - j + W].astype(jnp.float32)
            back = back + shifted[:, :, None] * conv_two[i, j].astype(jnp.float32)[None, None, :]
    grad_two = jnp.stack(grad_two).reshape(3, 3, C1)
    sig = jax.nn.sigmoid(pre)
    slope = (back * sig * (1.0 + pre * (1.0 - sig))).astype(jnp.bfloat16)
    slope_flat = slope.reshape(NH * W, C1)
    grad_one = []
    for i in range(3):
        for j in range(3):
            patch = padded[2 * i:2 * i + NH, 2 * j:2 * j + W, :].reshape(NH * W, STEPS)
            grad_one.append(lax.dot_general(patch, slope_flat, (((0,), (0,)), ((), ())), preferred_element_type=jnp.float32))
    grad_one = jnp.stack(grad_one).reshape(3, 3, STEPS, C1)
    grad_bias = lax.optimization_barrier(jnp.sum(slope_flat.astype(jnp.float32), axis=0))
    return (pred, grad_one, grad_bias, grad_two)

def normalized(grad):
    return grad / jnp.sqrt(jnp.mean(grad * grad) + 1e-06)

def reference(waves, dest_tile, pixel_bin, target, conv_one, bias_one, conv_two, bias_two):
    preds = []
    total_one = jnp.zeros((3, 3, STEPS, C1), jnp.float32)
    total_bias = jnp.zeros((C1,), jnp.float32)
    total_two = jnp.zeros((3, 3, C1), jnp.float32)
    for r in range(N_REP):
        pred, grad_one, grad_bias, grad_two = replica_terms(waves[r], dest_tile[r], pixel_bin[r], target[r], conv_one, bias_one, conv_two, bias_two)
        preds.append(pred)
        total_one = total_one + grad_one
        total_bias = total_bias + grad_bias
        total_two = total_two + grad_two
    return (jnp.stack(preds), normalized(total_one), normalized(total_bias), normalized(total_two))
```

```python
import functools

import jax
import jax.numpy as jnp
from jax import lax
from jax.experimental import pallas as pl
from jax.experimental.pallas import tpu as pltpu
from jax.sharding import PartitionSpec as P

CAP = 32
HALO = 4
CHUNKS = 4
LEVELS = 32000.0
MESH = pl.DeviceIdType.MESH
F32 = jnp.float32
BF16 = jnp.bfloat16


def iota(shape, dim):
    return lax.broadcasted_iota(jnp.int32, shape, dim)


def dot(a, b, dims=((1,), (0,))):
    return lax.dot_general(a, b, (dims, ((), ())), preferred_element_type=F32)


def repeat(count, body):
    if count <= 16:
        for n in range(count):
            body(n)
    else:

        def step(n, carry):
            body(n)
            return carry

        lax.fori_loop(0, count, step, 0)


def pair_rows(part):
    return 2 * part - 8


def small_row(n):
    return 8 * (n // 4) + (2 if n // 2 % 2 else 6) + n % 2


def exponent(largest):
    largest = jnp.maximum(jnp.max(largest, axis=0, keepdims=True), 2.0**-100)
    return jnp.ceil(jnp.log2(largest))


def encode(value, odd):
    last = value[-8:]
    row = iota(last.shape, 0)
    own = (row >= 4) == (odd == 1)
    inner = row - jnp.where(row >= 4, 4, 0)
    size = jnp.abs(last)
    largest = jnp.where(own, size, 0.0)
    for t in range(value.shape[0] // 8 - 1):
        largest = jnp.maximum(largest, jnp.abs(value[8 * t : 8 * t + 8]))
    one = exponent(largest)
    two = exponent(jnp.where(jnp.logical_or(own, inner < 2), 0.0, size))
    by_one = jnp.exp2(-one) * LEVELS
    by_two = jnp.exp2(-two) * LEVELS
    last = jnp.where(
        own, last * by_one, jnp.where(inner == 0, one, jnp.where(inner == 1, two, last * by_two))
    )
    if value.shape[0] > 8:
        last = jnp.concatenate([value[:-8] * by_one, last], axis=0)
    return jnp.round(last).astype(jnp.int32).astype(jnp.int16)


def decode(code, odd):
    value = code.astype(jnp.int32).astype(F32)
    last = value[-8:]
    own = (iota(last.shape, 0) >= 4) == (odd == 1)
    if isinstance(odd, int):
        one, two = (last[0:1], last[1:2]) if odd else (last[4:5], last[5:6])
    else:
        one = jnp.where(odd == 1, last[0:1], last[4:5])
        two = jnp.where(odd == 1, last[1:2], last[5:6])
    by_one = jnp.exp2(one) * (1.0 / LEVELS)
    last = last * jnp.where(own, by_one, jnp.exp2(two) * (1.0 / LEVELS))
    return jnp.concatenate([value[:-8] * by_one, last], axis=0) if value.shape[0] > 8 else last


def sum_shares(codes, odd):
    count = codes.shape[0]
    if count <= 16:
        out = decode(codes[0], odd)
        for s in range(1, count):
            out = out + decode(codes[s], odd)
        return out
    return lax.fori_loop(
        0, count, lambda s, out: out + decode(codes[s], odd), jnp.zeros(codes.shape[1:], F32)
    )


def step_kernel(
    tiles, reps, part,
    dest_hbm, bin_hbm, waves_hbm, target_hbm, w1_hbm, b1_hbm, w2_hbm, b2_hbm,
    pred_ref, out_ref,
    dest_ref, bin_ref, waves_ref, target_ref, w1_ref, b1_ref, w2_ref, b2_ref, l_sem,
    sendw, sendb, recvw, recvb, grid, wide, pre_s, hid_s, tlow, thigh, w2_s, taps, etap,
    full, pair, total, coded, recva, gathered,
    aw_send, aw_recv, ab_send, ab_recv, t_send, t_recv, g_send, g_recv,
    p_send, p_recv, s_send, s_recv, n_send, n_recv, f_send, f_recv,
):
    me = lax.axis_index("tile")
    rep = lax.axis_index("rep")
    rows, steps = waves_ref.shape
    height, width = target_ref.shape
    channels = b1_ref.shape[1]
    half = tiles // 2
    groups = half * reps
    core = lax.rem(me, 2)
    partner = me + 1 - 2 * core
    chip = rep * half + me // 2
    chunks = CHUNKS
    pixels = height * width
    tall = height + HALO

    def tile_peer(k):
        return lax.rem(me + k, tiles)

    def group_peer(k):
        q = lax.rem(chip + k, groups)
        return q, device_at(q)

    def device_at(q):
        return {"tile": 2 * lax.rem(q, half) + core, "rep": q // half}

    loads = [
        pltpu.make_async_copy(src, dst, l_sem.at[k])
        for k, (src, dst) in enumerate(
            [
                (dest_hbm, dest_ref), (bin_hbm, bin_ref), (waves_hbm, waves_ref), (target_hbm, target_ref),
                (w1_hbm, w1_ref), (b1_hbm, b1_ref), (w2_hbm, w2_ref), (b2_hbm, b2_ref),
            ]
        )
    ]
    for load in loads:
        load.start()

    barrier = pltpu.get_barrier_semaphore()

    def greet(k, carry):
        pl.semaphore_signal(barrier, inc=1, device_id={"tile": tile_peer(k), "rep": rep}, device_id_type=MESH)
        return carry

    lax.fori_loop(1, tiles, greet, 0)

    def greet_far(k, carry):
        pl.semaphore_signal(
            barrier,
            inc=1,
            device_id={"tile": 2 * lax.rem(k, half) + core, "rep": lax.rem(rep + 1 + k // half, reps)},
            device_id_type=MESH,
        )
        return carry

    lax.fori_loop(0, (reps - 1) * half, greet_far, 0)

    for load in loads[:4]:
        load.wait()

    hits = (iota((tiles, rows), 0) == dest_ref[...]).astype(F32)
    earlier = (iota((rows, rows), 0) < iota((rows, rows), 1)).astype(F32).astype(BF16)
    ranks = dot(hits.astype(BF16), earlier)
    rank = jnp.sum(hits * ranks, axis=0, keepdims=True)
    slot = jnp.sum(hits * (ranks + (CAP * iota((tiles, rows), 0)).astype(F32)), axis=0, keepdims=True)
    place = (iota((tiles * CAP, rows), 0).astype(F32) == slot).astype(F32).astype(BF16)
    sendw[...] = dot(place, waves_ref[...]).astype(BF16)
    lane = rank + (CAP * lax.rem(me, 4)).astype(F32)
    lanes = (iota((128, rows), 0).astype(F32) == lane).astype(F32).astype(BF16)
    bins = bin_ref[...]
    high = (bins // 32).astype(F32)
    low = (bins - 32 * (bins // 32)).astype(F32)
    named = 32.0 * dot((hits * high).astype(BF16), lanes, ((1,), (1,))) + dot(
        (hits * low).astype(BF16), lanes, ((1,), (1,))
    )
    for t in range(tiles):
        sendb[t] = named[t : t + 1, :]

    pl.semaphore_wait(barrier, tiles - 1 + (reps - 1) * half)

    def wave_copy(peer, source):
        return pltpu.make_async_remote_copy(
            src_ref=sendw.at[pl.ds(pl.multiple_of(peer * CAP, CAP), CAP)],
            dst_ref=recvw.at[pl.ds(pl.multiple_of(source * CAP, CAP), CAP)],
            send_sem=aw_send.at[peer],
            recv_sem=aw_recv.at[source],
            device_id={"tile": peer, "rep": rep},
            device_id_type=MESH,
        )

    def bin_copy(peer, source):
        return pltpu.make_async_remote_copy(
            src_ref=sendb.at[peer],
            dst_ref=recvb.at[source],
            send_sem=ab_send.at[peer],
            recv_sem=ab_recv.at[source],
            device_id={"tile": peer, "rep": rep},
            device_id_type=MESH,
        )

    def scatter(k, carry):
        peer = tile_peer(k)
        wave_copy(peer, me).start()
        bin_copy(peer, me).start()
        return carry

    lax.fori_loop(1, tiles, scatter, 0)

    up = jnp.minimum(me + 1, tiles - 1)
    down = jnp.maximum(me - 1, 0)
    span = HALO * width

    def target_copy(peer, dst, k):
        return pltpu.make_async_remote_copy(
            src_ref=target_ref, dst_ref=dst, send_sem=t_send.at[k], recv_sem=t_recv.at[k],
            device_id={"tile": peer, "rep": rep}, device_id_type=MESH,
        )

    def halo_copy(peer, src, dst, k):
        return pltpu.make_async_remote_copy(
            src_ref=grid.at[pl.ds(src, span)], dst_ref=grid.at[pl.ds(dst, span)],
            send_sem=g_send.at[k], recv_sem=g_recv.at[k],
            device_id={"tile": peer, "rep": rep}, device_id_type=MESH,
        )

    to_up = target_copy(up, tlow, 0)
    to_down = target_copy(down, thigh, 1)
    grid_up = halo_copy(up, span + pixels - span, 0, 0)
    grid_down = halo_copy(down, span, span + pixels, 1)
    has_up = me < tiles - 1
    has_down = me > 0

    @pl.when(has_up)
    def _():
        to_up.start()

    @pl.when(has_down)
    def _():
        to_down.start()

    @pl.when(jnp.logical_not(has_down))
    def _():
        grid[0:span, :] = jnp.zeros((span, steps), BF16)
        tlow[...] = jnp.zeros((height, width), F32)

    @pl.when(jnp.logical_not(has_up))
    def _():
        grid[span + pixels : span + pixels + span, :] = jnp.zeros((span, steps), BF16)
        thigh[...] = jnp.zeros((height, width), F32)

    own = pl.ds(pl.multiple_of(me * CAP, CAP), CAP)
    recvw[own, :] = sendw[own, :]
    recvb[me] = sendb[me]
    for load in loads[4:]:
        load.wait()
    w2_s[...] = jnp.zeros(w2_s.shape, F32)
    for i in range(3):
        w2_s[8 * i : 8 * i + 3, :] = w2_ref[i].astype(F32)
    w2 = w2_s[...].astype(BF16)

    def arrive(k, carry):
        peer = tile_peer(k)
        wave_copy(peer, peer).wait_recv()
        bin_copy(peer, peer).wait_recv()
        return carry

    lax.fori_loop(1, tiles, arrive, 0)

    names = []
    for q in range(tiles // 4):
        names.append(recvb[4 * q] + recvb[4 * q + 1] + recvb[4 * q + 2] + recvb[4 * q + 3])
    names = jnp.concatenate(names, axis=1)
    block = 256
    order = [0, pixels - block] + [s for s in range(block, pixels - block, block)]
    for start in order:
        wanted = (iota((block, tiles * CAP), 0) + start).astype(F32)
        onehot = (wanted == names).astype(F32).astype(BF16)
        grid[span + start : span + start + block, :] = dot(onehot, recvw[...]).astype(BF16)

    @pl.when(has_up)
    def _():
        grid_up.start()

    @pl.when(has_down)
    def _():
        grid_down.start()

    column = iota((width, steps), 0)

    def spread(y):
        line = grid[y * width : (y + 1) * width, :]
        value = line.astype(F32)
        left = jnp.where(column >= 2, pltpu.roll(value, 2, 0), 0.0)
        right = jnp.where(column < width - 2, pltpu.roll(value, width - 2, 0), 0.0)
        wide[y * width : (y + 1) * width, 0:steps] = left.astype(BF16)
        wide[y * width : (y + 1) * width, steps : 2 * steps] = line
        wide[y * width : (y + 1) * width, 2 * steps : 3 * steps] = right.astype(BF16)

    for y in range(HALO, HALO + height):
        spread(y)

    bias = b1_ref[...]

    def convolve(y):
        acc = jnp.zeros((2 * width, channels), F32) + bias
        for i in range(3):
            acc = acc + dot(wide[(y + 2 * i) * width : (y + 2 * i + 2) * width, :], w1_ref[i])
        sig = 1.0 / (1.0 + jnp.exp(-acc))
        hidden = acc * sig
        if y < 2:
            hidden = jnp.where(has_down, hidden, 0.0)
        if y >= height + 2:
            hidden = jnp.where(has_up, hidden, 0.0)
        hid_s[y * width : (y + 2) * width, :] = hidden.astype(BF16)
        if 2 <= y < height + 2:
            pre_s[(y - 2) * width : y * width, :] = sig * (1.0 + acc * (1.0 - sig))

    middle = [y for y in range(HALO, height, 2)]
    for y in middle:
        convolve(y)

    @pl.when(has_down)
    def _():
        grid_up.wait_recv()

    @pl.when(has_up)
    def _():
        grid_down.wait_recv()

    for y in list(range(HALO)) + list(range(HALO + height, 2 * HALO + height)):
        spread(y)

    for y in range(0, tall, 2):
        if y not in middle:
            convolve(y)

    each = dot(w2, hid_s[...], ((1,), (1,)))
    span2 = (height + 2) * width
    summed = each[0:8, 0:span2] + each[8:16, width : width + span2] + each[16:24, 2 * width : 2 * width + span2]
    taps[...] = jnp.zeros(taps.shape, F32)
    for y in range(height + 2):
        for j in range(3):
            taps[j, y : y + 1, :] = summed[j : j + 1, y * width : (y + 1) * width]
    tp = taps.shape[1]
    x_at = iota((tp, width), 1)
    y_at = iota((tp, width), 0)
    pred = (
        b2_ref[0]
        + jnp.where(x_at >= 1, pltpu.roll(taps[0], 1, 1), 0.0)
        + taps[1]
        + jnp.where(x_at < width - 1, pltpu.roll(taps[2], width - 1, 1), 0.0)
    )

    @pl.when(has_down)
    def _():
        to_up.wait_recv()

    @pl.when(has_up)
    def _():
        to_down.wait_recv()

    taps[3] = pred
    pred_ref[...] = taps[3, 1 : 1 + height, :]
    taps[4, 0:1, :] = tlow[height - 1 : height, :]
    taps[4, 1 : 1 + height, :] = target_ref[...]
    taps[4, 1 + height : 2 + height, :] = thigh[0:1, :]
    inside = jnp.logical_and(
        jnp.logical_or(y_at >= 1, has_down),
        jnp.logical_and(y_at < height + 2, jnp.logical_or(y_at < height + 1, has_up)),
    )
    error = jnp.where(inside, (pred - taps[4]) / reps, 0.0).astype(BF16).astype(F32)
    taps[0] = jnp.where(x_at < width - 1, pltpu.roll(error, width - 1, 1), 0.0)
    taps[1] = error
    taps[2] = jnp.where(x_at >= 1, pltpu.roll(error, 1, 1), 0.0)
    etap[...] = jnp.zeros(etap.shape, F32)
    for i in range(3):
        for j in range(3):
            for y in range(height):
                etap[8 * i + j : 8 * i + j + 1, y * width : (y + 1) * width] = taps[j, y + 2 - i : y + 3 - i, :]
    errors = etap[...].astype(BF16)

    mine = hid_s[2 * width : 2 * width + pixels, :]
    grad_two = dot(errors, mine)
    back = dot(errors, w2, ((0,), (0,)))
    slope = (back * pre_s[...]).astype(BF16)
    grad_bias = dot(jnp.ones((8, pixels), BF16), slope)
    piece = steps // 2
    data = 9 * piece
    spare = pair_rows(part) * (groups // 2)
    for h in range(2):
        if spare > data:
            full[h, data:spare, :] = jnp.zeros((spare - data, channels), F32)
        full[h, spare:, :] = jnp.zeros((full.shape[1] - spare, channels), F32)
        for n in range(10):
            at = spare + small_row(n)
            full[h, at : at + 1, :] = grad_two[8 * (n // 3) + n % 3 :, :][0:1] if n < 9 else grad_bias[0:1]
    slab = spare // chunks

    def swap(a):
        rows_a = pl.ds(a * slab, slab) if a < chunks else pl.ds(spare, full.shape[1] - spare)
        return pltpu.make_async_remote_copy(
            src_ref=full.at[1 - core, rows_a], dst_ref=pair.at[rows_a],
            send_sem=p_send.at[a], recv_sem=p_recv.at[a],
            device_id={"tile": partner, "rep": rep}, device_id_type=MESH,
        )

    swap(chunks).start()
    started = 0
    for i in range(3):
        start = (2 + 2 * i) * width
        g = dot(wide[start : start + pixels, :], slope, ((0,), (0,)))
        for j in range(3):
            k = 3 * i + j
            for h in range(2):
                full[h, k * piece : (k + 1) * piece, :] = g[j * steps + h * piece : j * steps + (h + 1) * piece, :]
        while started < chunks and ((started + 1) * slab <= 3 * (i + 1) * piece or i == 2):
            swap(started).start()
            started += 1

    def share_copy(q, source):
        return pltpu.make_async_remote_copy(
            src_ref=coded.at[q], dst_ref=recva.at[source],
            send_sem=s_send.at[q], recv_sem=s_recv.at[source],
            device_id=device_at(q), device_id_type=MESH,
        )

    whole = part - 8
    per_pair = pair_rows(part)
    top = iota((8, channels), 0) < 4

    def hand_out(p):
        rows_p = pl.ds(p * per_pair, per_pair)
        rows_s = pl.ds(spare + p * 8, 8)
        x = full[core, rows_p, :] + pair[rows_p, :]
        extra = full[core, rows_s, :] + pair[rows_s, :]
        for odd in range(2):
            q = 2 * p + odd
            mixed = x[whole : whole + 8]
            mixed = jnp.where(top, extra, mixed) if odd else jnp.where(top, mixed, extra)
            value = x[whole + 8 :] if odd else x[:whole]
            value = jnp.concatenate([value, mixed], axis=0) if whole else mixed

            @pl.when(chip == q)
            def _():
                total[...] = value

            @pl.when(chip != q)
            def _():
                coded[q] = encode(value, odd)
                share_copy(q, chip).start()

    swap(chunks).wait_recv()
    pairs_each = groups // 2 // chunks
    for a in range(chunks):
        swap(a).wait_recv()
        repeat(pairs_each, lambda n: hand_out(a * pairs_each + n))

    def arrived(k):
        share_copy(lax.rem(chip + k, groups), lax.rem(chip + groups - k, groups)).wait_recv()

    repeat(groups - 1, lambda n: arrived(n + 1))
    parity = lax.rem(chip, 2)
    recva[chip] = jnp.zeros(recva.shape[1:], recva.dtype)
    total[...] = total[...] + sum_shares(recva, parity)
    gathered[core, chip] = encode(total[...], parity)

    def spread_copy(device, source):
        return pltpu.make_async_remote_copy(
            src_ref=gathered.at[core, chip], dst_ref=gathered.at[core, source],
            send_sem=n_send.at[source], recv_sem=n_recv.at[source], device_id=device, device_id_type=MESH,
        )

    def spread_start(k, carry):
        q, device = group_peer(k)
        pltpu.make_async_remote_copy(
            src_ref=gathered.at[core, chip], dst_ref=gathered.at[core, chip],
            send_sem=n_send.at[q], recv_sem=n_recv.at[chip], device_id=device, device_id_type=MESH,
        ).start()
        return carry

    lax.fori_loop(1, groups, spread_start, 0)

    def forward(q, which):
        return pltpu.make_async_remote_copy(
            src_ref=gathered.at[which, q], dst_ref=gathered.at[which, q],
            send_sem=f_send.at[q], recv_sem=f_recv.at[q],
            device_id={"tile": partner, "rep": rep}, device_id_type=MESH,
        )

    forward(chip, core).start()

    def pass_on(k, carry):
        q, device = group_peer(groups - k)
        spread_copy(device, q).wait_recv()
        forward(q, core).start()
        return carry

    lax.fori_loop(1, groups, pass_on, 0)

    def finish(q, carry):
        forward(q, 1 - core).wait_recv()
        return carry

    lax.fori_loop(0, groups, finish, 0)

    out_ref[...] = gathered[...]

    @pl.when(has_up)
    def _():
        to_up.wait_send()
        grid_up.wait_send()

    @pl.when(has_down)
    def _():
        to_down.wait_send()
        grid_down.wait_send()

    def sent(k, carry):
        peer = tile_peer(k)
        wave_copy(peer, me).wait_send()
        bin_copy(peer, me).wait_send()
        return carry

    lax.fori_loop(1, tiles, sent, 0)
    for a in range(chunks + 1):
        swap(a).wait_send()

    def handed(k):
        share_copy(lax.rem(chip + k, groups), chip).wait_send()

    repeat(groups - 1, lambda n: handed(n + 1))

    def shared(k, carry):
        q, device = group_peer(k)
        spread_copy(device, q).wait_send()
        return carry

    lax.fori_loop(1, groups, shared, 0)

    def passed(q, carry):
        forward(q, core).wait_send()
        return carry

    lax.fori_loop(0, groups, passed, 0)


def finish_kernel(
    pred_ref, gathered, pred_out, u1_out, ub_out, u2_out, u1, ub, u2, sem
):
    groups, part, channels = gathered.shape[1:]
    steps = u1.shape[2]
    piece = steps // 2
    whole = part - 8
    per_pair = pair_rows(part)
    copies = [
        pltpu.make_async_copy(src, dst, sem.at[k])
        for k, (src, dst) in enumerate([(pred_ref, pred_out), (u1, u1_out), (ub, ub_out), (u2, u2_out)])
    ]
    copies[0].start()
    top = iota((8, channels), 0) < 4
    smalls = []
    square = jnp.zeros((8, channels), F32)
    for h in range(2):
        for p in range(-(-9 * piece // per_pair)):
            even = decode(gathered[h, 2 * p], 0)
            odd = decode(gathered[h, 2 * p + 1], 1)
            tiles = [even[8 * t : 8 * t + 8] for t in range(whole // 8)]
            tiles.append(jnp.where(top, even[whole:], odd[whole:]))
            tiles += [odd[8 * t : 8 * t + 8] for t in range(whole // 8)]
            if h == 0 and p < 3:
                smalls.append(jnp.where(top, odd[whole:], even[whole:]))
            for t, tile in enumerate(tiles):
                at = p * per_pair + 8 * t
                if at < 9 * piece:
                    k, r = at // piece, h * piece + at % piece
                    u1[k // 3, k % 3, r : r + 8, :] = tile
                    square = square + tile * tile
    scale = 1.0 / jnp.sqrt(jnp.sum(square) / (9 * steps * channels) + 1e-06)
    u1[...] = u1[...] * scale
    copies[1].start()
    rows = []
    for n in range(10):
        at = small_row(n)
        rows.append(smalls[at // 8][at % 8 : at % 8 + 1])
    two = jnp.zeros((1, channels), F32)
    for row in rows[:9]:
        two = two + row * row
    scale = 1.0 / jnp.sqrt(jnp.sum(two) / (9 * channels) + 1e-06)
    for n in range(9):
        u2[n // 3, n % 3 : n % 3 + 1, :] = rows[n] * scale
    ub[...] = rows[9] / jnp.sqrt(jnp.sum(rows[9] * rows[9]) / channels + 1e-06)
    copies[2].start()
    copies[3].start()
    for copy in copies:
        copy.wait()


def on_device(tiles, reps, waves, dest_tile, pixel_bin, target, conv_one, bias_one, conv_two, bias_two):
    rows, steps = waves.shape[1:]
    height, width = target.shape[1:]
    channels = conv_one.shape[3]
    pixels = height * width
    groups = tiles // 2 * reps
    units = -(-9 * (steps // 8) // groups) // 2 * 2 + 1
    part = 4 * units + 4
    padded = (pair_rows(part) + 8) * (groups // 2)
    hbm = pl.BlockSpec(memory_space=pltpu.HBM)
    tp = -(-(height + 2) // 8) * 8
    dma = pltpu.SemaphoreType.DMA
    vmem = pl.BlockSpec(memory_space=pltpu.VMEM)
    pred, gathered = pl.pallas_call(
        functools.partial(step_kernel, tiles, reps, part),
        out_shape=(
            pltpu.VMEM((height, width), F32),
            pltpu.VMEM((2, groups, part, channels), jnp.int16),
        ),
        in_specs=[hbm] * 8,
        out_specs=(vmem,) * 2,
        scratch_shapes=[
            pltpu.VMEM((1, rows), jnp.int32),
            pltpu.VMEM((1, rows), jnp.int32),
            pltpu.VMEM((rows, steps), BF16),
            pltpu.VMEM((height, width), F32),
            pltpu.VMEM((3, 3 * steps, channels), BF16),
            pltpu.VMEM((1, channels), F32),
            pltpu.VMEM((3, 3, channels), BF16),
            pltpu.SMEM((1,), F32),
            dma((8,)),
            pltpu.VMEM((tiles * CAP, steps), BF16),
            pltpu.VMEM((tiles, 1, 128), F32),
            pltpu.VMEM((tiles * CAP, steps), BF16),
            pltpu.VMEM((tiles, 1, 128), F32),
            pltpu.VMEM(((height + 2 * HALO) * width, steps), BF16),
            pltpu.VMEM(((height + 2 * HALO) * width, 3 * steps), BF16),
            pltpu.VMEM((pixels, channels), F32),
            pltpu.VMEM(((height + HALO) * width, channels), BF16),
            pltpu.VMEM((height, width), F32),
            pltpu.VMEM((height, width), F32),
            pltpu.VMEM((24, channels), F32),
            pltpu.VMEM((5, tp, width), F32),
            pltpu.VMEM((24, pixels), F32),
            pltpu.VMEM((2, padded, channels), F32),
            pltpu.VMEM((padded, channels), F32),
            pltpu.VMEM((part, channels), F32),
            pltpu.VMEM((groups, part, channels), jnp.int16),
            pltpu.VMEM((groups, part, channels), jnp.int16),
            pltpu.VMEM((2, groups, part, channels), jnp.int16),
            dma((tiles,)), dma((tiles,)), dma((tiles,)), dma((tiles,)),
            dma((2,)), dma((2,)), dma((2,)), dma((2,)),
            dma((CHUNKS + 1,)), dma((CHUNKS + 1,)), dma((groups,)), dma((groups,)),
            dma((groups,)), dma((groups,)), dma((groups,)), dma((groups,)),
        ],
        compiler_params=pltpu.CompilerParams(
            collective_id=0, has_side_effects=True, vmem_limit_bytes=60 * 1024 * 1024
        ),
        name="step",
    )(
        dest_tile.reshape(1, rows), pixel_bin, waves[0], target[0],
        conv_one.reshape(3, 3 * steps, channels), bias_one.reshape(1, channels), conv_two, bias_two,
    )
    pred, one, bias, two = pl.pallas_call(
        finish_kernel,
        out_shape=(
            jax.ShapeDtypeStruct((height, width), F32),
            jax.ShapeDtypeStruct((3, 3, steps, channels), F32),
            jax.ShapeDtypeStruct((1, channels), F32),
            jax.ShapeDtypeStruct((3, 3, channels), F32),
        ),
        in_specs=[vmem] * 2,
        out_specs=(hbm,) * 4,
        scratch_shapes=[
            pltpu.VMEM((3, 3, steps, channels), F32),
            pltpu.VMEM((1, channels), F32),
            pltpu.VMEM((3, 3, channels), F32),
            dma((4,)),
        ],
        name="finish",
    )(pltpu.with_memory_space_constraint(pred, pltpu.VMEM), pltpu.with_memory_space_constraint(gathered, pltpu.VMEM))
    return pred[None], one, bias[0], two


def solution(mesh):
    placed = (
        P("rep", "tile", None),
        P("rep", "tile", None),
        P("rep", "tile"),
        P("rep", "tile", None),
        P(),
        P(),
        P(),
        P(),
    )
    return jax.shard_map(
        functools.partial(on_device, mesh.shape["tile"], mesh.shape["rep"]),
        mesh=mesh,
        in_specs=placed,
        out_specs=(P("rep", "tile", None), P(), P(), P()),
        check_vma=False,
    )
```

```python
import functools

import jax
import jax.numpy as jnp
from jax import lax
from jax.experimental import pallas as pl
from jax.experimental.pallas import tpu as pltpu
from jax.sharding import PartitionSpec as P

CAP = 32
HALO = 4
CHUNKS = 4
LEVELS = 32000.0
MESH = pl.DeviceIdType.MESH
F32 = jnp.float32
BF16 = jnp.bfloat16


def iota(shape, dim):
    return lax.broadcasted_iota(jnp.int32, shape, dim)


def dot(a, b, dims=((1,), (0,))):
    return lax.dot_general(a, b, (dims, ((), ())), preferred_element_type=F32)


def repeat(count, body):
    if count <= 16:
        for n in range(count):
            body(n)
    else:

        def step(n, carry):
            body(n)
            return carry

        lax.fori_loop(0, count, step, 0)


def pair_rows(part):
    return 2 * part - 8


def small_row(n):
    return 8 * (n // 4) + (2 if n // 2 % 2 else 6) + n % 2


def exponent(largest):
    largest = jnp.maximum(jnp.max(largest, axis=0, keepdims=True), 2.0**-100)
    return jnp.ceil(jnp.log2(largest))


def encode(value, odd):
    last = value[-8:]
    row = iota(last.shape, 0)
    own = (row >= 4) == (odd == 1)
    inner = row - jnp.where(row >= 4, 4, 0)
    size = jnp.abs(last)
    largest = jnp.where(own, size, 0.0)
    for t in range(value.shape[0] // 8 - 1):
        largest = jnp.maximum(largest, jnp.abs(value[8 * t : 8 * t + 8]))
    one = exponent(largest)
    two = exponent(jnp.where(jnp.logical_or(own, inner < 2), 0.0, size))
    by_one = jnp.exp2(-one) * LEVELS
    by_two = jnp.exp2(-two) * LEVELS
    last = jnp.where(
        own, last * by_one, jnp.where(inner == 0, one, jnp.where(inner == 1, two, last * by_two))
    )
    if value.shape[0] > 8:
        last = jnp.concatenate([value[:-8] * by_one, last], axis=0)
    return jnp.round(last).astype(jnp.int32).astype(jnp.int16)


def decode(code, odd):
    value = code.astype(jnp.int32).astype(F32)
    last = value[-8:]
    own = (iota(last.shape, 0) >= 4) == (odd == 1)
    if isinstance(odd, int):
        one, two = (last[0:1], last[1:2]) if odd else (last[4:5], last[5:6])
    else:
        one = jnp.where(odd == 1, last[0:1], last[4:5])
        two = jnp.where(odd == 1, last[1:2], last[5:6])
    by_one = jnp.exp2(one) * (1.0 / LEVELS)
    last = last * jnp.where(own, by_one, jnp.exp2(two) * (1.0 / LEVELS))
    return jnp.concatenate([value[:-8] * by_one, last], axis=0) if value.shape[0] > 8 else last


def sum_shares(codes, odd):
    count = codes.shape[0]
    if count <= 16:
        out = decode(codes[0], odd)
        for s in range(1, count):
            out = out + decode(codes[s], odd)
        return out
    return lax.fori_loop(
        0, count, lambda s, out: out + decode(codes[s], odd), jnp.zeros(codes.shape[1:], F32)
    )


def holder(strip):
    pair, chip = strip // 4, strip // 2
    turned = 2 * pair + lax.rem(chip + pair, 2)
    return 2 * turned + lax.rem(strip, 2)


def step_kernel(
    tiles, reps, part,
    dest_hbm, bin_hbm, waves_hbm, target_hbm, w1_hbm, b1_hbm, w2_hbm, b2_hbm,
    pred_ref, out_ref,
    dest_ref, bin_ref, waves_ref, target_ref, w1_ref, b1_ref, w2_ref, b2_ref, l_sem,
    sendw, sendb, recvw, recvb, grid, wide, pre_s, hid_s, acc_s, tlow, thigh, tmid, pout, pin, w2_s, taps, etap,
    full, pair, total, coded, recva, gathered,
    aw_send, aw_recv, ab_send, ab_recv, t_send, t_recv, g_send, g_recv,
    p_send, p_recv, s_send, s_recv, n_send, n_recv, f_send, f_recv,
):
    me = lax.axis_index("tile")
    rep = lax.axis_index("rep")
    rows, steps = waves_ref.shape
    height, width = target_ref.shape
    channels = b1_ref.shape[1]
    half = tiles // 2
    groups = half * reps
    core = lax.rem(me, 2)
    partner = me + 1 - 2 * core
    chip = rep * half + me // 2
    strip = holder(me)
    chunks = CHUNKS
    pixels = height * width
    tall = height + HALO

    def tile_peer(k):
        return lax.rem(me + k, tiles)

    def group_peer(k):
        q = lax.rem(chip + k, groups)
        return q, device_at(q)

    def device_at(q):
        return {"tile": 2 * lax.rem(q, half) + core, "rep": q // half}

    loads = [
        pltpu.make_async_copy(src, dst, l_sem.at[k])
        for k, (src, dst) in enumerate(
            [
                (dest_hbm, dest_ref), (bin_hbm, bin_ref), (waves_hbm, waves_ref), (target_hbm, target_ref),
                (w1_hbm, w1_ref), (b1_hbm, b1_ref), (w2_hbm, w2_ref), (b2_hbm, b2_ref),
            ]
        )
    ]
    for load in loads:
        load.start()

    barrier = pltpu.get_barrier_semaphore()

    def greet(k, carry):
        pl.semaphore_signal(barrier, inc=1, device_id={"tile": tile_peer(k), "rep": rep}, device_id_type=MESH)
        return carry

    repeat(tiles - 1, lambda n: greet(n + 1, 0))

    def greet_far(k, carry):
        pl.semaphore_signal(
            barrier,
            inc=1,
            device_id={"tile": 2 * lax.rem(k, half) + core, "rep": lax.rem(rep + 1 + k // half, reps)},
            device_id_type=MESH,
        )
        return carry

    repeat((reps - 1) * half, lambda n: greet_far(n, 0))

    for load in loads[:4]:
        load.wait()

    hits = (iota((tiles, rows), 0) == dest_ref[...]).astype(F32)
    earlier = (iota((rows, rows), 0) < iota((rows, rows), 1)).astype(F32).astype(BF16)
    ranks = dot(hits.astype(BF16), earlier)
    rank = jnp.sum(hits * ranks, axis=0, keepdims=True)
    slot = jnp.sum(hits * (ranks + (CAP * iota((tiles, rows), 0)).astype(F32)), axis=0, keepdims=True)
    place = (iota((tiles * CAP, rows), 0).astype(F32) == slot).astype(F32).astype(BF16)
    sendw[...] = dot(place, waves_ref[...]).astype(BF16)
    lane = rank + (CAP * lax.rem(me, 4)).astype(F32)
    lanes = (iota((128, rows), 0).astype(F32) == lane).astype(F32).astype(BF16)
    bins = bin_ref[...]
    high = (bins // 32).astype(F32)
    low = (bins - 32 * (bins // 32)).astype(F32)
    named = 32.0 * dot((hits * high).astype(BF16), lanes, ((1,), (1,))) + dot(
        (hits * low).astype(BF16), lanes, ((1,), (1,))
    )
    for t in range(tiles):
        sendb[t] = named[t : t + 1, :]

    pl.semaphore_wait(barrier, tiles - 1 + (reps - 1) * half)

    def wave_copy(peer, source):
        return pltpu.make_async_remote_copy(
            src_ref=sendw.at[pl.ds(pl.multiple_of(holder(peer) * CAP, CAP), CAP)],
            dst_ref=recvw.at[pl.ds(pl.multiple_of(source * CAP, CAP), CAP)],
            send_sem=aw_send.at[peer],
            recv_sem=aw_recv.at[source],
            device_id={"tile": peer, "rep": rep},
            device_id_type=MESH,
        )

    def bin_copy(peer, source):
        return pltpu.make_async_remote_copy(
            src_ref=sendb.at[holder(peer)],
            dst_ref=recvb.at[source],
            send_sem=ab_send.at[peer],
            recv_sem=ab_recv.at[source],
            device_id={"tile": peer, "rep": rep},
            device_id_type=MESH,
        )

    def scatter(k, carry):
        peer = tile_peer(k)
        wave_copy(peer, me).start()
        bin_copy(peer, me).start()
        return carry

    lax.fori_loop(1, tiles, scatter, 0)

    def target_copy(peer, dst, k):
        return pltpu.make_async_remote_copy(
            src_ref=target_ref, dst_ref=dst, send_sem=t_send.at[k], recv_sem=t_recv.at[k],
            device_id={"tile": peer, "rep": rep}, device_id_type=MESH,
        )

    has_up = strip < tiles - 1
    has_down = strip > 0
    up = holder(jnp.minimum(strip + 1, tiles - 1))
    down = holder(jnp.maximum(strip - 1, 0))
    span = HALO * width
    step_px = 2 * width

    def halo_copy(peer, src, dst, k):
        return pltpu.make_async_remote_copy(
            src_ref=grid.at[pl.ds(src * width, step_px)], dst_ref=grid.at[pl.ds(dst * width, step_px)],
            send_sem=g_send.at[k], recv_sem=g_recv.at[k],
            device_id={"tile": peer, "rep": rep}, device_id_type=MESH,
        )

    to_up = target_copy(holder(jnp.minimum(me + 1, tiles - 1)), tlow, 0)
    to_down = target_copy(holder(jnp.maximum(me - 1, 0)), thigh, 1)
    to_mid = target_copy(strip, tmid, 2)
    grid_up = [halo_copy(up, height + 2, 2, 0), halo_copy(up, height, 0, 1)]
    grid_down = [halo_copy(down, HALO, height + HALO, 2), halo_copy(down, HALO + 2, height + HALO + 2, 3)]

    @pl.when(me < tiles - 1)
    def _():
        to_up.start()

    @pl.when(me > 0)
    def _():
        to_down.start()

    @pl.when(strip != me)
    def _():
        to_mid.start()

    @pl.when(strip == me)
    def _():
        tmid[...] = target_ref[...]

    @pl.when(jnp.logical_not(has_down))
    def _():
        grid[0:span, :] = jnp.zeros((span, steps), BF16)
        tlow[...] = jnp.zeros((height, width), F32)

    @pl.when(jnp.logical_not(has_up))
    def _():
        grid[span + pixels : span + pixels + span, :] = jnp.zeros((span, steps), BF16)
        thigh[...] = jnp.zeros((height, width), F32)

    own = pl.ds(pl.multiple_of(me * CAP, CAP), CAP)
    recvw[own, :] = sendw[pl.ds(pl.multiple_of(strip * CAP, CAP), CAP), :]
    recvb[me] = sendb[strip]
    for load in loads[4:]:
        load.wait()
    w2_s[...] = jnp.zeros(w2_s.shape, F32)
    for i in range(3):
        w2_s[8 * i : 8 * i + 3, :] = w2_ref[i].astype(F32)
    w2 = w2_s[...].astype(BF16)

    def arrive(k, carry):
        peer = tile_peer(k)
        wave_copy(peer, peer).wait_recv()
        bin_copy(peer, peer).wait_recv()
        return carry

    lax.fori_loop(1, tiles, arrive, 0)

    names = []
    for q in range(tiles // 4):
        names.append(recvb[4 * q] + recvb[4 * q + 1] + recvb[4 * q + 2] + recvb[4 * q + 3])
    names = jnp.concatenate(names, axis=1)
    stages = [(height - 2, has_up, grid_up[0]), (0, has_down, grid_down[0])]
    stages += [(height - 4, has_up, grid_up[1]), (2, has_down, grid_down[1])]
    stages += [(y, None, None) for y in range(HALO, height - HALO, 2)]
    for y, there, copy in stages:
        wanted = (iota((step_px, tiles * CAP), 0) + y * width).astype(F32)
        onehot = (wanted == names).astype(F32).astype(BF16)
        grid[span + y * width : span + y * width + step_px, :] = dot(onehot, recvw[...]).astype(BF16)
        if copy is not None:
            pl.when(there)(copy.start)

    column = iota((width, steps), 0)

    def spread(y):
        line = grid[y * width : (y + 1) * width, :]
        value = line.astype(F32)
        left = jnp.where(column >= 2, pltpu.roll(value, 2, 0), 0.0)
        right = jnp.where(column < width - 2, pltpu.roll(value, width - 2, 0), 0.0)
        wide[y * width : (y + 1) * width, 0:steps] = left.astype(BF16)
        wide[y * width : (y + 1) * width, steps : 2 * steps] = line
        wide[y * width : (y + 1) * width, 2 * steps : 3 * steps] = right.astype(BF16)

    for y in range(HALO, HALO + height):
        spread(y)

    bias = b1_ref[...]

    def convolve(y, terms, first, last):
        acc = jnp.zeros((step_px, channels), F32) + bias if first else acc_s[y * width : (y + 2) * width, :]
        for i in terms:
            acc = acc + dot(wide[(y + 2 * i) * width : (y + 2 * i + 2) * width, :], w1_ref[i])
        if not last:
            acc_s[y * width : (y + 2) * width, :] = acc
            return
        sig = 1.0 / (1.0 + jnp.exp(-acc))
        hidden = acc * sig
        if y < 2:
            hidden = jnp.where(has_down, hidden, 0.0)
        if y >= height + 2:
            hidden = jnp.where(has_up, hidden, 0.0)
        hid_s[y * width : (y + 2) * width, :] = hidden.astype(BF16)
        if 2 <= y < height + 2:
            pre_s[(y - 2) * width : y * width, :] = sig * (1.0 + acc * (1.0 - sig))

    begun = set()

    def advance(rows):
        for y in range(0, tall, 2):
            terms = [i for i in range(3) if y + 2 * i in rows]
            if terms:
                done[y] = done.get(y, 0) + len(terms)
                convolve(y, terms, y not in begun, done[y] == 3)
                begun.add(y)

    done = {}
    advance(range(HALO, HALO + height, 2))
    for k in range(2):

        @pl.when(has_down)
        def _():
            grid_up[k].wait_recv()

        @pl.when(has_up)
        def _():
            grid_down[k].wait_recv()

        fresh = [2 - 2 * k, height + HALO + 2 * k]
        for y in fresh:
            spread(y)
            spread(y + 1)
        advance(fresh)

    each = dot(w2, hid_s[...], ((1,), (1,)))
    span2 = (height + 2) * width
    summed = each[0:8, 0:span2] + each[8:16, width : width + span2] + each[16:24, 2 * width : 2 * width + span2]
    taps[...] = jnp.zeros(taps.shape, F32)
    for y in range(height + 2):
        for j in range(3):
            taps[j, y : y + 1, :] = summed[j : j + 1, y * width : (y + 1) * width]
    tp = taps.shape[1]
    x_at = iota((tp, width), 1)
    y_at = iota((tp, width), 0)
    pred = (
        b2_ref[...]
        + jnp.where(x_at >= 1, pltpu.roll(taps[0], 1, 1), 0.0)
        + taps[1]
        + jnp.where(x_at < width - 1, pltpu.roll(taps[2], width - 1, 1), 0.0)
    )

    @pl.when(has_down)
    def _():
        to_up.wait_recv()

    @pl.when(has_up)
    def _():
        to_down.wait_recv()

    @pl.when(strip != me)
    def _():
        to_mid.wait_recv()

    taps[3] = pred
    pout[...] = taps[3, 1 : 1 + height, :]
    hand_over = pltpu.make_async_remote_copy(
        src_ref=pout, dst_ref=pin, send_sem=t_send.at[3], recv_sem=t_recv.at[3],
        device_id={"tile": strip, "rep": rep}, device_id_type=MESH,
    )
    pl.when(strip != me)(hand_over.start)
    taps[4, 0:1, :] = tlow[height - 1 : height, :]
    taps[4, 1 : 1 + height, :] = tmid[...]
    taps[4, 1 + height : 2 + height, :] = thigh[0:1, :]
    inside = jnp.logical_and(
        jnp.logical_or(y_at >= 1, has_down),
        jnp.logical_and(y_at < height + 2, jnp.logical_or(y_at < height + 1, has_up)),
    )
    error = jnp.where(inside, (pred - taps[4]) / reps, 0.0).astype(BF16).astype(F32)
    taps[0] = jnp.where(x_at < width - 1, pltpu.roll(error, width - 1, 1), 0.0)
    taps[1] = error
    taps[2] = jnp.where(x_at >= 1, pltpu.roll(error, 1, 1), 0.0)
    etap[...] = jnp.zeros(etap.shape, F32)
    for i in range(3):
        for j in range(3):
            for y in range(height):
                etap[8 * i + j : 8 * i + j + 1, y * width : (y + 1) * width] = taps[j, y + 2 - i : y + 3 - i, :]
    errors = etap[...].astype(BF16)

    mine = hid_s[2 * width : 2 * width + pixels, :]
    grad_two = dot(errors, mine)
    back = dot(errors, w2, ((0,), (0,)))
    slope = (back * pre_s[...]).astype(BF16)
    grad_bias = dot(jnp.ones((8, pixels), BF16), slope)
    piece = steps // 2
    data = 9 * piece
    spare = pair_rows(part) * (groups // 2)
    for h in range(2):
        if spare > data:
            full[h, data:spare, :] = jnp.zeros((spare - data, channels), F32)
        full[h, spare:, :] = jnp.zeros((full.shape[1] - spare, channels), F32)
        for n in range(10):
            at = spare + small_row(n)
            full[h, at : at + 1, :] = grad_two[8 * (n // 3) + n % 3 :, :][0:1] if n < 9 else grad_bias[0:1]
    slab = spare // chunks

    def swap(a):
        rows_a = pl.ds(a * slab, slab) if a < chunks else pl.ds(spare, full.shape[1] - spare)
        return pltpu.make_async_remote_copy(
            src_ref=full.at[1 - core, rows_a], dst_ref=pair.at[rows_a],
            send_sem=p_send.at[a], recv_sem=p_recv.at[a],
            device_id={"tile": partner, "rep": rep}, device_id_type=MESH,
        )

    swap(chunks).start()
    started = 0
    for i in range(3):
        start = (2 + 2 * i) * width
        g = dot(wide[start : start + pixels, :], slope, ((0,), (0,)))
        for j in range(3):
            k = 3 * i + j
            for h in range(2):
                full[h, k * piece : (k + 1) * piece, :] = g[j * steps + h * piece : j * steps + (h + 1) * piece, :]
        while started < chunks and ((started + 1) * slab <= 3 * (i + 1) * piece or i == 2):
            swap(started).start()
            started += 1

    def share_copy(q, source):
        return pltpu.make_async_remote_copy(
            src_ref=coded.at[q], dst_ref=recva.at[source],
            send_sem=s_send.at[q], recv_sem=s_recv.at[source],
            device_id=device_at(q), device_id_type=MESH,
        )

    whole = part - 8
    per_pair = pair_rows(part)
    top = iota((8, channels), 0) < 4

    def hand_out(p):
        rows_p = pl.ds(p * per_pair, per_pair)
        rows_s = pl.ds(spare + p * 8, 8)
        x = full[core, rows_p, :] + pair[rows_p, :]
        extra = full[core, rows_s, :] + pair[rows_s, :]
        for odd in range(2):
            q = 2 * p + odd
            mixed = x[whole : whole + 8]
            mixed = jnp.where(top, extra, mixed) if odd else jnp.where(top, mixed, extra)
            value = x[whole + 8 :] if odd else x[:whole]
            value = jnp.concatenate([value, mixed], axis=0) if whole else mixed

            @pl.when(chip == q)
            def _():
                total[...] = value

            @pl.when(chip != q)
            def _():
                coded[q] = encode(value, odd)
                share_copy(q, chip).start()

    swap(chunks).wait_recv()
    pairs_each = groups // 2 // chunks
    for a in range(chunks):
        swap(a).wait_recv()
        repeat(pairs_each, lambda n: hand_out(a * pairs_each + n))

    def arrived(k):
        share_copy(lax.rem(chip + k, groups), lax.rem(chip + groups - k, groups)).wait_recv()

    repeat(groups - 1, lambda n: arrived(n + 1))
    parity = lax.rem(chip, 2)
    recva[chip] = jnp.zeros(recva.shape[1:], recva.dtype)
    total[...] = total[...] + sum_shares(recva, parity)
    gathered[core, chip] = encode(total[...], parity)

    def spread_copy(device, source):
        return pltpu.make_async_remote_copy(
            src_ref=gathered.at[core, chip], dst_ref=gathered.at[core, source],
            send_sem=n_send.at[source], recv_sem=n_recv.at[source], device_id=device, device_id_type=MESH,
        )

    def spread_start(k, carry):
        q, device = group_peer(k)
        pltpu.make_async_remote_copy(
            src_ref=gathered.at[core, chip], dst_ref=gathered.at[core, chip],
            send_sem=n_send.at[q], recv_sem=n_recv.at[chip], device_id=device, device_id_type=MESH,
        ).start()
        return carry

    lax.fori_loop(1, groups, spread_start, 0)

    def forward(q, which):
        return pltpu.make_async_remote_copy(
            src_ref=gathered.at[which, q], dst_ref=gathered.at[which, q],
            send_sem=f_send.at[q], recv_sem=f_recv.at[q],
            device_id={"tile": partner, "rep": rep}, device_id_type=MESH,
        )

    forward(chip, core).start()

    def pass_on(k, carry):
        q, device = group_peer(groups - k)
        spread_copy(device, q).wait_recv()
        forward(q, core).start()
        return carry

    lax.fori_loop(1, groups, pass_on, 0)

    def finish(q, carry):
        forward(q, 1 - core).wait_recv()
        return carry

    lax.fori_loop(0, groups, finish, 0)

    out_ref[...] = gathered[...]

    @pl.when(strip == me)
    def _():
        pred_ref[...] = pout[...]

    @pl.when(strip != me)
    def _():
        hand_over.wait()
        pred_ref[...] = pin[...]
        to_mid.wait_send()

    @pl.when(me < tiles - 1)
    def _():
        to_up.wait_send()

    @pl.when(me > 0)
    def _():
        to_down.wait_send()

    @pl.when(has_up)
    def _():
        for copy in grid_up:
            copy.wait_send()

    @pl.when(has_down)
    def _():
        for copy in grid_down:
            copy.wait_send()

    def sent(k, carry):
        peer = tile_peer(k)
        wave_copy(peer, me).wait_send()
        bin_copy(peer, me).wait_send()
        return carry

    lax.fori_loop(1, tiles, sent, 0)
    for a in range(chunks + 1):
        swap(a).wait_send()

    def handed(k):
        share_copy(lax.rem(chip + k, groups), chip).wait_send()

    repeat(groups - 1, lambda n: handed(n + 1))

    def shared(k, carry):
        q, device = group_peer(k)
        spread_copy(device, q).wait_send()
        return carry

    lax.fori_loop(1, groups, shared, 0)

    def passed(q, carry):
        forward(q, core).wait_send()
        return carry

    lax.fori_loop(0, groups, passed, 0)


def finish_kernel(
    pred_ref, gathered, pred_out, u1_out, ub_out, u2_out, u1, ub, u2, sem
):
    groups, part, channels = gathered.shape[1:]
    steps = u1.shape[2]
    piece = steps // 2
    whole = part - 8
    per_pair = pair_rows(part)
    copies = [
        pltpu.make_async_copy(src, dst, sem.at[k])
        for k, (src, dst) in enumerate([(pred_ref, pred_out), (u1, u1_out), (ub, ub_out), (u2, u2_out)])
    ]
    copies[0].start()
    top = iota((8, channels), 0) < 4
    smalls = []
    square = jnp.zeros((8, channels), F32)
    for h in range(2):
        for p in range(-(-9 * piece // per_pair)):
            even = decode(gathered[h, 2 * p], 0)
            odd = decode(gathered[h, 2 * p + 1], 1)
            tiles = [even[8 * t : 8 * t + 8] for t in range(whole // 8)]
            tiles.append(jnp.where(top, even[whole:], odd[whole:]))
            tiles += [odd[8 * t : 8 * t + 8] for t in range(whole // 8)]
            if h == 0 and p < 3:
                smalls.append(jnp.where(top, odd[whole:], even[whole:]))
            for t, tile in enumerate(tiles):
                at = p * per_pair + 8 * t
                if at < 9 * piece:
                    k, r = at // piece, h * piece + at % piece
                    u1[k // 3, k % 3, r : r + 8, :] = tile
                    square = square + tile * tile
    scale = 1.0 / jnp.sqrt(jnp.sum(square) / (9 * steps * channels) + 1e-06)
    u1[...] = u1[...] * scale
    copies[1].start()
    rows = []
    for n in range(10):
        at = small_row(n)
        rows.append(smalls[at // 8][at % 8 : at % 8 + 1])
    two = jnp.zeros((1, channels), F32)
    for row in rows[:9]:
        two = two + row * row
    scale = 1.0 / jnp.sqrt(jnp.sum(two) / (9 * channels) + 1e-06)
    for n in range(9):
        u2[n // 3, n % 3 : n % 3 + 1, :] = rows[n] * scale
    ub[...] = rows[9] / jnp.sqrt(jnp.sum(rows[9] * rows[9]) / channels + 1e-06)
    copies[2].start()
    copies[3].start()
    for copy in copies:
        copy.wait()


def on_device(tiles, reps, waves, dest_tile, pixel_bin, target, conv_one, bias_one, conv_two, bias_two):
    rows, steps = waves.shape[1:]
    height, width = target.shape[1:]
    channels = conv_one.shape[3]
    pixels = height * width
    groups = tiles // 2 * reps
    units = -(-9 * (steps // 8) // groups) // 2 * 2 + 1
    part = 4 * units + 4
    padded = (pair_rows(part) + 8) * (groups // 2)
    hbm = pl.BlockSpec(memory_space=pltpu.HBM)
    tp = -(-(height + 2) // 8) * 8
    dma = pltpu.SemaphoreType.DMA
    vmem = pl.BlockSpec(memory_space=pltpu.VMEM)
    pred, gathered = pl.pallas_call(
        functools.partial(step_kernel, tiles, reps, part),
        out_shape=(
            pltpu.VMEM((height, width), F32),
            pltpu.VMEM((2, groups, part, channels), jnp.int16),
        ),
        in_specs=[hbm] * 8,
        out_specs=(vmem,) * 2,
        scratch_shapes=[
            pltpu.VMEM((1, rows), jnp.int32),
            pltpu.VMEM((1, rows), jnp.int32),
            pltpu.VMEM((rows, steps), BF16),
            pltpu.VMEM((height, width), F32),
            pltpu.VMEM((3, 3 * steps, channels), BF16),
            pltpu.VMEM((1, channels), F32),
            pltpu.VMEM((3, 3, channels), BF16),
            pltpu.VMEM((1, 1), F32),
            dma((8,)),
            pltpu.VMEM((tiles * CAP, steps), BF16),
            pltpu.VMEM((tiles, 1, 128), F32),
            pltpu.VMEM((tiles * CAP, steps), BF16),
            pltpu.VMEM((tiles, 1, 128), F32),
            pltpu.VMEM(((height + 2 * HALO) * width, steps), BF16),
            pltpu.VMEM(((height + 2 * HALO) * width, 3 * steps), BF16),
            pltpu.VMEM((pixels, channels), F32),
            pltpu.VMEM(((height + HALO) * width, channels), BF16),
            pltpu.VMEM(((height + HALO) * width, channels), F32),
            pltpu.VMEM((height, width), F32),
            pltpu.VMEM((height, width), F32),
            pltpu.VMEM((height, width), F32),
            pltpu.VMEM((height, width), F32),
            pltpu.VMEM((height, width), F32),
            pltpu.VMEM((24, channels), F32),
            pltpu.VMEM((5, tp, width), F32),
            pltpu.VMEM((24, pixels), F32),
            pltpu.VMEM((2, padded, channels), F32),
            pltpu.VMEM((padded, channels), F32),
            pltpu.VMEM((part, channels), F32),
            pltpu.VMEM((groups, part, channels), jnp.int16),
            pltpu.VMEM((groups, part, channels), jnp.int16),
            pltpu.VMEM((2, groups, part, channels), jnp.int16),
            dma((tiles,)), dma((tiles,)), dma((tiles,)), dma((tiles,)),
            dma((4,)), dma((4,)), dma((4,)), dma((4,)),
            dma((CHUNKS + 1,)), dma((CHUNKS + 1,)), dma((groups,)), dma((groups,)),
            dma((groups,)), dma((groups,)), dma((groups,)), dma((groups,)),
        ],
        compiler_params=pltpu.CompilerParams(
            collective_id=0, has_side_effects=True, vmem_limit_bytes=60 * 1024 * 1024
        ),
        name="step",
    )(
        dest_tile.reshape(1, rows), pixel_bin, waves[0], target[0],
        conv_one.reshape(3, 3 * steps, channels), bias_one.reshape(1, channels), conv_two, bias_two.reshape(1, 1),
    )
    pred, one, bias, two = pl.pallas_call(
        finish_kernel,
        out_shape=(
            jax.ShapeDtypeStruct((height, width), F32),
            jax.ShapeDtypeStruct((3, 3, steps, channels), F32),
            jax.ShapeDtypeStruct((1, channels), F32),
            jax.ShapeDtypeStruct((3, 3, channels), F32),
        ),
        in_specs=[vmem] * 2,
        out_specs=(hbm,) * 4,
        scratch_shapes=[
            pltpu.VMEM((3, 3, steps, channels), F32),
            pltpu.VMEM((1, channels), F32),
            pltpu.VMEM((3, 3, channels), F32),
            dma((4,)),
        ],
        name="finish",
    )(pltpu.with_memory_space_constraint(pred, pltpu.VMEM), pltpu.with_memory_space_constraint(gathered, pltpu.VMEM))
    return pred[None], one, bias[0], two


def solution(mesh):
    placed = (
        P("rep", "tile", None),
        P("rep", "tile", None),
        P("rep", "tile"),
        P("rep", "tile", None),
        P(),
        P(),
        P(),
        P(),
    )
    return jax.shard_map(
        functools.partial(on_device, mesh.shape["tile"], mesh.shape["rep"]),
        mesh=mesh,
        in_specs=placed,
        out_specs=(P("rep", "tile", None), P(), P(), P()),
        check_vma=False,
    )
```

```python
import functools

import jax
import jax.numpy as jnp
from jax import lax
from jax.experimental import pallas as pl
from jax.experimental.pallas import tpu as pltpu
from jax.sharding import PartitionSpec as P

CAP = 32
HALO = 4
CHUNKS = 4
LEVELS = 32000.0
MESH = pl.DeviceIdType.MESH
F32 = jnp.float32
BF16 = jnp.bfloat16


def iota(shape, dim):
    return lax.broadcasted_iota(jnp.int32, shape, dim)


def dot(a, b, dims=((1,), (0,))):
    return lax.dot_general(a, b, (dims, ((), ())), preferred_element_type=F32)


def repeat(count, body):
    if count <= 16:
        for n in range(count):
            body(n)
    else:

        def step(n, carry):
            body(n)
            return carry

        lax.fori_loop(0, count, step, 0)


def pair_rows(part):
    return 2 * part - 8


def small_row(n):
    return 8 * (n // 4) + (2 if n // 2 % 2 else 6) + n % 2


def exponent(largest):
    largest = jnp.maximum(jnp.max(largest, axis=0, keepdims=True), 2.0**-100)
    return jnp.ceil(jnp.log2(largest))


def encode(value, odd):
    last = value[-8:]
    row = iota(last.shape, 0)
    own = (row >= 4) == (odd == 1)
    inner = row - jnp.where(row >= 4, 4, 0)
    size = jnp.abs(last)
    largest = jnp.where(own, size, 0.0)
    for t in range(value.shape[0] // 8 - 1):
        largest = jnp.maximum(largest, jnp.abs(value[8 * t : 8 * t + 8]))
    one = exponent(largest)
    two = exponent(jnp.where(jnp.logical_or(own, inner < 2), 0.0, size))
    by_one = jnp.exp2(-one) * LEVELS
    by_two = jnp.exp2(-two) * LEVELS
    last = jnp.where(
        own, last * by_one, jnp.where(inner == 0, one, jnp.where(inner == 1, two, last * by_two))
    )
    if value.shape[0] > 8:
        last = jnp.concatenate([value[:-8] * by_one, last], axis=0)
    return jnp.round(last).astype(jnp.int32).astype(jnp.int16)


def decode(code, odd):
    value = code.astype(jnp.int32).astype(F32)
    last = value[-8:]
    own = (iota(last.shape, 0) >= 4) == (odd == 1)
    if isinstance(odd, int):
        one, two = (last[0:1], last[1:2]) if odd else (last[4:5], last[5:6])
    else:
        one = jnp.where(odd == 1, last[0:1], last[4:5])
        two = jnp.where(odd == 1, last[1:2], last[5:6])
    by_one = jnp.exp2(one) * (1.0 / LEVELS)
    last = last * jnp.where(own, by_one, jnp.exp2(two) * (1.0 / LEVELS))
    return jnp.concatenate([value[:-8] * by_one, last], axis=0) if value.shape[0] > 8 else last


def sum_shares(codes, odd):
    count = codes.shape[0]
    if count <= 16:
        out = decode(codes[0], odd)
        for s in range(1, count):
            out = out + decode(codes[s], odd)
        return out
    return lax.fori_loop(
        0, count, lambda s, out: out + decode(codes[s], odd), jnp.zeros(codes.shape[1:], F32)
    )


def holder(strip):
    pair, chip = strip // 4, strip // 2
    turned = 2 * pair + lax.rem(chip + pair, 2)
    return 2 * turned + lax.rem(strip, 2)


def step_kernel(
    tiles, reps, part,
    dest_hbm, bin_hbm, waves_hbm, target_hbm, w1_hbm, b1_hbm, w2_hbm, b2_hbm,
    pred_ref, raw_ref, extra_ref,
    dest_ref, bin_ref, waves_ref, target_ref, w1_ref, b1_ref, w2_ref, b2_ref, l_sem,
    sendw, sendb, recvw, recvb, grid, wide, pre_s, hid_s, acc_s, tlow, thigh, tmid, pout, pin, w2_s, taps, etap,
    full, pair, total, coded, recva, gathered, square,
    aw_send, aw_recv, ab_send, ab_recv, t_send, t_recv, g_send, g_recv,
    p_send, p_recv, s_send, s_recv, n_send, n_recv, f_send, f_recv,
):
    me = lax.axis_index("tile")
    rep = lax.axis_index("rep")
    rows, steps = waves_ref.shape
    height, width = target_ref.shape
    channels = b1_ref.shape[1]
    half = tiles // 2
    groups = half * reps
    core = lax.rem(me, 2)
    partner = me + 1 - 2 * core
    chip = rep * half + me // 2
    strip = holder(me)
    chunks = CHUNKS
    pixels = height * width
    tall = height + HALO

    def tile_peer(k):
        return lax.rem(me + k, tiles)

    def group_peer(k):
        q = lax.rem(chip + k, groups)
        return q, device_at(q)

    def device_at(q):
        return {"tile": 2 * lax.rem(q, half) + core, "rep": q // half}

    loads = [
        pltpu.make_async_copy(src, dst, l_sem.at[k])
        for k, (src, dst) in enumerate(
            [
                (dest_hbm, dest_ref), (bin_hbm, bin_ref), (waves_hbm, waves_ref), (target_hbm, target_ref),
                (w1_hbm, w1_ref), (b1_hbm, b1_ref), (w2_hbm, w2_ref), (b2_hbm, b2_ref),
            ]
        )
    ]
    for load in loads:
        load.start()

    barrier = pltpu.get_barrier_semaphore()

    def greet(k, carry):
        pl.semaphore_signal(barrier, inc=1, device_id={"tile": tile_peer(k), "rep": rep}, device_id_type=MESH)
        return carry

    repeat(tiles - 1, lambda n: greet(n + 1, 0))

    def greet_far(k, carry):
        pl.semaphore_signal(
            barrier,
            inc=1,
            device_id={"tile": 2 * lax.rem(k, half) + core, "rep": lax.rem(rep + 1 + k // half, reps)},
            device_id_type=MESH,
        )
        return carry

    repeat((reps - 1) * half, lambda n: greet_far(n, 0))

    for load in loads[:4]:
        load.wait()

    hits = (iota((tiles, rows), 0) == dest_ref[...]).astype(F32)
    earlier = (iota((rows, rows), 0) < iota((rows, rows), 1)).astype(F32).astype(BF16)
    ranks = dot(hits.astype(BF16), earlier)
    rank = jnp.sum(hits * ranks, axis=0, keepdims=True)
    slot = jnp.sum(hits * (ranks + (CAP * iota((tiles, rows), 0)).astype(F32)), axis=0, keepdims=True)
    place = (iota((tiles * CAP, rows), 0).astype(F32) == slot).astype(F32).astype(BF16)
    sendw[...] = dot(place, waves_ref[...]).astype(BF16)
    lane = rank + (CAP * lax.rem(me, 4)).astype(F32)
    lanes = (iota((128, rows), 0).astype(F32) == lane).astype(F32).astype(BF16)
    bins = bin_ref[...]
    high = (bins // 32).astype(F32)
    low = (bins - 32 * (bins // 32)).astype(F32)
    named = 32.0 * dot((hits * high).astype(BF16), lanes, ((1,), (1,))) + dot(
        (hits * low).astype(BF16), lanes, ((1,), (1,))
    )
    for t in range(tiles):
        sendb[t] = named[t : t + 1, :]

    pl.semaphore_wait(barrier, tiles - 1 + (reps - 1) * half)

    def wave_copy(peer, source):
        return pltpu.make_async_remote_copy(
            src_ref=sendw.at[pl.ds(pl.multiple_of(holder(peer) * CAP, CAP), CAP)],
            dst_ref=recvw.at[pl.ds(pl.multiple_of(source * CAP, CAP), CAP)],
            send_sem=aw_send.at[peer],
            recv_sem=aw_recv.at[source],
            device_id={"tile": peer, "rep": rep},
            device_id_type=MESH,
        )

    def bin_copy(peer, source):
        return pltpu.make_async_remote_copy(
            src_ref=sendb.at[holder(peer)],
            dst_ref=recvb.at[source],
            send_sem=ab_send.at[peer],
            recv_sem=ab_recv.at[source],
            device_id={"tile": peer, "rep": rep},
            device_id_type=MESH,
        )

    def scatter(k, carry):
        peer = tile_peer(k)
        wave_copy(peer, me).start()
        bin_copy(peer, me).start()
        return carry

    lax.fori_loop(1, tiles, scatter, 0)

    def target_copy(peer, dst, k):
        return pltpu.make_async_remote_copy(
            src_ref=target_ref, dst_ref=dst, send_sem=t_send.at[k], recv_sem=t_recv.at[k],
            device_id={"tile": peer, "rep": rep}, device_id_type=MESH,
        )

    has_up = strip < tiles - 1
    has_down = strip > 0
    up = holder(jnp.minimum(strip + 1, tiles - 1))
    down = holder(jnp.maximum(strip - 1, 0))
    span = HALO * width
    step_px = 2 * width

    def halo_copy(peer, src, dst, k):
        return pltpu.make_async_remote_copy(
            src_ref=grid.at[pl.ds(src * width, step_px)], dst_ref=grid.at[pl.ds(dst * width, step_px)],
            send_sem=g_send.at[k], recv_sem=g_recv.at[k],
            device_id={"tile": peer, "rep": rep}, device_id_type=MESH,
        )

    to_up = target_copy(holder(jnp.minimum(me + 1, tiles - 1)), tlow, 0)
    to_down = target_copy(holder(jnp.maximum(me - 1, 0)), thigh, 1)
    to_mid = target_copy(strip, tmid, 2)
    grid_up = [halo_copy(up, height + 2, 2, 0), halo_copy(up, height, 0, 1)]
    grid_down = [halo_copy(down, HALO, height + HALO, 2), halo_copy(down, HALO + 2, height + HALO + 2, 3)]

    @pl.when(me < tiles - 1)
    def _():
        to_up.start()

    @pl.when(me > 0)
    def _():
        to_down.start()

    @pl.when(strip != me)
    def _():
        to_mid.start()

    @pl.when(strip == me)
    def _():
        tmid[...] = target_ref[...]

    @pl.when(jnp.logical_not(has_down))
    def _():
        grid[0:span, :] = jnp.zeros((span, steps), BF16)
        tlow[...] = jnp.zeros((height, width), F32)

    @pl.when(jnp.logical_not(has_up))
    def _():
        grid[span + pixels : span + pixels + span, :] = jnp.zeros((span, steps), BF16)
        thigh[...] = jnp.zeros((height, width), F32)

    own = pl.ds(pl.multiple_of(me * CAP, CAP), CAP)
    recvw[own, :] = sendw[pl.ds(pl.multiple_of(strip * CAP, CAP), CAP), :]
    recvb[me] = sendb[strip]
    for load in loads[4:]:
        load.wait()
    w2_s[...] = jnp.zeros(w2_s.shape, F32)
    for i in range(3):
        w2_s[8 * i : 8 * i + 3, :] = w2_ref[i].astype(F32)
    w2 = w2_s[...].astype(BF16)

    def arrive(k, carry):
        peer = tile_peer(k)
        wave_copy(peer, peer).wait_recv()
        bin_copy(peer, peer).wait_recv()
        return carry

    lax.fori_loop(1, tiles, arrive, 0)

    names = []
    for q in range(tiles // 4):
        names.append(recvb[4 * q] + recvb[4 * q + 1] + recvb[4 * q + 2] + recvb[4 * q + 3])
    names = jnp.concatenate(names, axis=1)
    stages = [(height - 2, has_up, grid_up[0]), (0, has_down, grid_down[0])]
    stages += [(height - 4, has_up, grid_up[1]), (2, has_down, grid_down[1])]
    stages += [(y, None, None) for y in range(HALO, height - HALO, 2)]
    for y, there, copy in stages:
        wanted = (iota((step_px, tiles * CAP), 0) + y * width).astype(F32)
        onehot = (wanted == names).astype(F32).astype(BF16)
        grid[span + y * width : span + y * width + step_px, :] = dot(onehot, recvw[...]).astype(BF16)
        if copy is not None:
            pl.when(there)(copy.start)

    column = iota((width, steps), 0)

    def spread(y):
        line = grid[y * width : (y + 1) * width, :]
        value = line.astype(F32)
        left = jnp.where(column >= 2, pltpu.roll(value, 2, 0), 0.0)
        right = jnp.where(column < width - 2, pltpu.roll(value, width - 2, 0), 0.0)
        wide[y * width : (y + 1) * width, 0:steps] = left.astype(BF16)
        wide[y * width : (y + 1) * width, steps : 2 * steps] = line
        wide[y * width : (y + 1) * width, 2 * steps : 3 * steps] = right.astype(BF16)

    for y in range(HALO, HALO + height):
        spread(y)

    bias = b1_ref[...]

    def convolve(y, terms, first, last):
        acc = jnp.zeros((step_px, channels), F32) + bias if first else acc_s[y * width : (y + 2) * width, :]
        for i in terms:
            acc = acc + dot(wide[(y + 2 * i) * width : (y + 2 * i + 2) * width, :], w1_ref[i])
        if not last:
            acc_s[y * width : (y + 2) * width, :] = acc
            return
        sig = 1.0 / (1.0 + jnp.exp(-acc))
        hidden = acc * sig
        if y < 2:
            hidden = jnp.where(has_down, hidden, 0.0)
        if y >= height + 2:
            hidden = jnp.where(has_up, hidden, 0.0)
        hid_s[y * width : (y + 2) * width, :] = hidden.astype(BF16)
        if 2 <= y < height + 2:
            pre_s[(y - 2) * width : y * width, :] = sig * (1.0 + acc * (1.0 - sig))

    begun = set()

    def advance(rows):
        for y in range(0, tall, 2):
            terms = [i for i in range(3) if y + 2 * i in rows]
            if terms:
                done[y] = done.get(y, 0) + len(terms)
                convolve(y, terms, y not in begun, done[y] == 3)
                begun.add(y)

    done = {}
    advance(range(HALO, HALO + height, 2))
    for k in range(2):

        @pl.when(has_down)
        def _():
            grid_up[k].wait_recv()

        @pl.when(has_up)
        def _():
            grid_down[k].wait_recv()

        fresh = [2 - 2 * k, height + HALO + 2 * k]
        for y in fresh:
            spread(y)
            spread(y + 1)
        advance(fresh)

    each = dot(w2, hid_s[...], ((1,), (1,)))
    span2 = (height + 2) * width
    summed = each[0:8, 0:span2] + each[8:16, width : width + span2] + each[16:24, 2 * width : 2 * width + span2]
    taps[...] = jnp.zeros(taps.shape, F32)
    for y in range(height + 2):
        for j in range(3):
            taps[j, y : y + 1, :] = summed[j : j + 1, y * width : (y + 1) * width]
    tp = taps.shape[1]
    x_at = iota((tp, width), 1)
    y_at = iota((tp, width), 0)
    pred = (
        b2_ref[...]
        + jnp.where(x_at >= 1, pltpu.roll(taps[0], 1, 1), 0.0)
        + taps[1]
        + jnp.where(x_at < width - 1, pltpu.roll(taps[2], width - 1, 1), 0.0)
    )

    @pl.when(has_down)
    def _():
        to_up.wait_recv()

    @pl.when(has_up)
    def _():
        to_down.wait_recv()

    @pl.when(strip != me)
    def _():
        to_mid.wait_recv()

    taps[3] = pred
    pout[...] = taps[3, 1 : 1 + height, :]
    hand_over = pltpu.make_async_remote_copy(
        src_ref=pout, dst_ref=pin, send_sem=t_send.at[3], recv_sem=t_recv.at[3],
        device_id={"tile": strip, "rep": rep}, device_id_type=MESH,
    )
    pl.when(strip != me)(hand_over.start)
    taps[4, 0:1, :] = tlow[height - 1 : height, :]
    taps[4, 1 : 1 + height, :] = tmid[...]
    taps[4, 1 + height : 2 + height, :] = thigh[0:1, :]
    inside = jnp.logical_and(
        jnp.logical_or(y_at >= 1, has_down),
        jnp.logical_and(y_at < height + 2, jnp.logical_or(y_at < height + 1, has_up)),
    )
    error = jnp.where(inside, (pred - taps[4]) / reps, 0.0).astype(BF16).astype(F32)
    taps[0] = jnp.where(x_at < width - 1, pltpu.roll(error, width - 1, 1), 0.0)
    taps[1] = error
    taps[2] = jnp.where(x_at >= 1, pltpu.roll(error, 1, 1), 0.0)
    etap[...] = jnp.zeros(etap.shape, F32)
    for i in range(3):
        for j in range(3):
            for y in range(height):
                etap[8 * i + j : 8 * i + j + 1, y * width : (y + 1) * width] = taps[j, y + 2 - i : y + 3 - i, :]
    errors = etap[...].astype(BF16)

    mine = hid_s[2 * width : 2 * width + pixels, :]
    grad_two = dot(errors, mine)
    back = dot(errors, w2, ((0,), (0,)))
    slope = (back * pre_s[...]).astype(BF16)
    grad_bias = dot(jnp.ones((8, pixels), BF16), slope)
    piece = steps // 2
    data = 9 * piece
    spare = pair_rows(part) * (groups // 2)
    for h in range(2):
        if spare > data:
            full[h, data:spare, :] = jnp.zeros((spare - data, channels), F32)
        full[h, spare:, :] = jnp.zeros((full.shape[1] - spare, channels), F32)
        for n in range(10):
            at = spare + small_row(n)
            full[h, at : at + 1, :] = grad_two[8 * (n // 3) + n % 3 :, :][0:1] if n < 9 else grad_bias[0:1]
    slab = spare // chunks

    def swap(a):
        rows_a = pl.ds(a * slab, slab) if a < chunks else pl.ds(spare, full.shape[1] - spare)
        return pltpu.make_async_remote_copy(
            src_ref=full.at[1 - core, rows_a], dst_ref=pair.at[rows_a],
            send_sem=p_send.at[a], recv_sem=p_recv.at[a],
            device_id={"tile": partner, "rep": rep}, device_id_type=MESH,
        )

    swap(chunks).start()
    started = 0
    for i in range(3):
        start = (2 + 2 * i) * width
        g = dot(wide[start : start + pixels, :], slope, ((0,), (0,)))
        for j in range(3):
            k = 3 * i + j
            for h in range(2):
                full[h, k * piece : (k + 1) * piece, :] = g[j * steps + h * piece : j * steps + (h + 1) * piece, :]
        while started < chunks and ((started + 1) * slab <= 3 * (i + 1) * piece or i == 2):
            swap(started).start()
            started += 1

    def share_copy(q, source):
        return pltpu.make_async_remote_copy(
            src_ref=coded.at[q], dst_ref=recva.at[source],
            send_sem=s_send.at[q], recv_sem=s_recv.at[source],
            device_id=device_at(q), device_id_type=MESH,
        )

    whole = part - 8
    per_pair = pair_rows(part)
    top = iota((8, channels), 0) < 4

    def hand_out(p):
        rows_p = pl.ds(p * per_pair, per_pair)
        rows_s = pl.ds(spare + p * 8, 8)
        x = full[core, rows_p, :] + pair[rows_p, :]
        extra = full[core, rows_s, :] + pair[rows_s, :]
        for odd in range(2):
            q = 2 * p + odd
            mixed = x[whole : whole + 8]
            mixed = jnp.where(top, extra, mixed) if odd else jnp.where(top, mixed, extra)
            value = x[whole + 8 :] if odd else x[:whole]
            value = jnp.concatenate([value, mixed], axis=0) if whole else mixed

            @pl.when(chip == q)
            def _():
                total[...] = value

            @pl.when(chip != q)
            def _():
                coded[q] = encode(value, odd)
                share_copy(q, chip).start()

    swap(chunks).wait_recv()
    pairs_each = groups // 2 // chunks
    for a in range(chunks):
        swap(a).wait_recv()
        repeat(pairs_each, lambda n: hand_out(a * pairs_each + n))

    def arrived(k):
        share_copy(lax.rem(chip + k, groups), lax.rem(chip + groups - k, groups)).wait_recv()

    repeat(groups - 1, lambda n: arrived(n + 1))
    parity = lax.rem(chip, 2)
    recva[chip] = jnp.zeros(recva.shape[1:], recva.dtype)
    total[...] = total[...] + sum_shares(recva, parity)
    gathered[core, chip] = encode(total[...], parity)

    def spread_copy(device, source):
        return pltpu.make_async_remote_copy(
            src_ref=gathered.at[core, chip], dst_ref=gathered.at[core, source],
            send_sem=n_send.at[source], recv_sem=n_recv.at[source], device_id=device, device_id_type=MESH,
        )

    def spread_start(k, carry):
        q, device = group_peer(k)
        pltpu.make_async_remote_copy(
            src_ref=gathered.at[core, chip], dst_ref=gathered.at[core, chip],
            send_sem=n_send.at[q], recv_sem=n_recv.at[chip], device_id=device, device_id_type=MESH,
        ).start()
        return carry

    repeat(groups - 1, lambda n: spread_start(n + 1, 0))

    def forward(q, which):
        return pltpu.make_async_remote_copy(
            src_ref=gathered.at[which, q], dst_ref=gathered.at[which, q],
            send_sem=f_send.at[q], recv_sem=f_recv.at[q],
            device_id={"tile": partner, "rep": rep}, device_id_type=MESH,
        )

    forward(chip, core).start()

    @pl.when(strip == me)
    def _():
        pred_ref[...] = pout[...]

    @pl.when(strip != me)
    def _():
        to_mid.wait_send()
        hand_over.wait()
        pred_ref[...] = pin[...]

    @pl.when(me < tiles - 1)
    def _():
        to_up.wait_send()

    @pl.when(me > 0)
    def _():
        to_down.wait_send()

    @pl.when(has_up)
    def _():
        for copy in grid_up:
            copy.wait_send()

    @pl.when(has_down)
    def _():
        for copy in grid_down:
            copy.wait_send()

    def sent(k, carry):
        peer = tile_peer(k)
        wave_copy(peer, me).wait_send()
        bin_copy(peer, me).wait_send()
        return carry

    lax.fori_loop(1, tiles, sent, 0)
    for a in range(chunks + 1):
        swap(a).wait_send()

    def handed(k):
        share_copy(lax.rem(chip + k, groups), chip).wait_send()

    repeat(groups - 1, lambda n: handed(n + 1))

    square[...] = jnp.zeros(square.shape, F32)
    count = 9 * piece

    def keep(h, p):
        even = decode(gathered[h, 2 * p], 0)
        odd = decode(gathered[h, 2 * p + 1], 1)
        tiles = [even[8 * t : 8 * t + 8] for t in range(whole // 8)]
        tiles.append(jnp.where(top, even[whole:], odd[whole:]))
        tiles += [odd[8 * t : 8 * t + 8] for t in range(whole // 8)]
        total_sq = square[...]
        for t, tile in enumerate(tiles):
            at = p * per_pair + 8 * t
            k, r = at // piece, at % piece
            raw_ref[k, pl.ds(pl.multiple_of(h * piece + r, 8), 8), :] = tile
            total_sq = total_sq + tile * tile
        square[...] = total_sq

    def keep_pair(h, p):
        if isinstance(p, int):
            if p * per_pair < count:
                keep(h, p)
        else:
            pl.when(p * per_pair < count)(lambda: keep(h, p))

    def take(p):
        for q in (2 * p, 2 * p + 1):

            @pl.when(chip != q)
            def _():
                spread_copy(device_at(q), q).wait_recv()
                forward(q, core).start()

        keep_pair(core, p)

    repeat(groups // 2, take)

    def shared(k, carry):
        q, device = group_peer(k)
        spread_copy(device, q).wait_send()
        return carry

    repeat(groups - 1, lambda n: shared(n + 1, 0))

    def fetch(p):
        for q in (2 * p, 2 * p + 1):
            forward(q, 1 - core).wait_recv()
        keep_pair(1 - core, p)

    repeat(groups // 2, fetch)
    extra_ref[10:16, :] = jnp.zeros((6, channels), F32) + 1.0 / jnp.sqrt(
        jnp.sum(square[...]) / (9 * steps * channels) + 1e-06
    )
    smalls = []
    for p in range(3):
        smalls.append(jnp.where(top, decode(gathered[0, 2 * p + 1], 1)[whole:], decode(gathered[0, 2 * p], 0)[whole:]))
    rows = []
    for n in range(10):
        at = small_row(n)
        rows.append(smalls[at // 8][at % 8 : at % 8 + 1])
    two = jnp.zeros((1, channels), F32)
    for row in rows[:9]:
        two = two + row * row
    scale_two = 1.0 / jnp.sqrt(jnp.sum(two) / (9 * channels) + 1e-06)
    for n in range(9):
        extra_ref[n : n + 1, :] = rows[n] * scale_two
    extra_ref[9:10, :] = rows[9] / jnp.sqrt(jnp.sum(rows[9] * rows[9]) / channels + 1e-06)

    def passed(q, carry):
        forward(q, core).wait_send()
        return carry

    repeat(groups, lambda q: passed(q, 0))


def finish_kernel(pred_ref, raw_ref, extra_ref, pred_out, u1_out, ub_out, u2_out, u1, ub, u2, sem):
    ub[...] = extra_ref[9:10, :]
    for n in range(9):
        u2[n // 3, n % 3 : n % 3 + 1, :] = extra_ref[n : n + 1, :]
    copies = [
        pltpu.make_async_copy(src, dst, sem.at[k])
        for k, (src, dst) in enumerate([(pred_ref, pred_out), (ub, ub_out), (u2, u2_out)])
    ]
    for copy in copies:
        copy.start()
    scale = extra_ref[10:11, :]
    for k in range(9):
        u1[k] = raw_ref[k] * scale
        copies.append(pltpu.make_async_copy(u1.at[k], u1_out.at[k // 3, k % 3], sem.at[3 + k]))
        copies[-1].start()
    for copy in copies:
        copy.wait()


def on_device(tiles, reps, waves, dest_tile, pixel_bin, target, conv_one, bias_one, conv_two, bias_two):
    rows, steps = waves.shape[1:]
    height, width = target.shape[1:]
    channels = conv_one.shape[3]
    pixels = height * width
    groups = tiles // 2 * reps
    units = -(-9 * (steps // 8) // groups) // 2 * 2 + 1
    part = 4 * units + 4
    padded = (pair_rows(part) + 8) * (groups // 2)
    hbm = pl.BlockSpec(memory_space=pltpu.HBM)
    tp = -(-(height + 2) // 8) * 8
    dma = pltpu.SemaphoreType.DMA
    vmem = pl.BlockSpec(memory_space=pltpu.VMEM)
    held = pl.pallas_call(
        functools.partial(step_kernel, tiles, reps, part),
        out_shape=(
            pltpu.VMEM((height, width), F32),
            pltpu.VMEM((9, steps, channels), F32),
            pltpu.VMEM((16, channels), F32),
        ),
        in_specs=[hbm] * 8,
        out_specs=(vmem,) * 3,
        scratch_shapes=[
            pltpu.VMEM((1, rows), jnp.int32),
            pltpu.VMEM((1, rows), jnp.int32),
            pltpu.VMEM((rows, steps), BF16),
            pltpu.VMEM((height, width), F32),
            pltpu.VMEM((3, 3 * steps, channels), BF16),
            pltpu.VMEM((1, channels), F32),
            pltpu.VMEM((3, 3, channels), BF16),
            pltpu.VMEM((1, 1), F32),
            dma((8,)),
            pltpu.VMEM((tiles * CAP, steps), BF16),
            pltpu.VMEM((tiles, 1, 128), F32),
            pltpu.VMEM((tiles * CAP, steps), BF16),
            pltpu.VMEM((tiles, 1, 128), F32),
            pltpu.VMEM(((height + 2 * HALO) * width, steps), BF16),
            pltpu.VMEM(((height + 2 * HALO) * width, 3 * steps), BF16),
            pltpu.VMEM((pixels, channels), F32),
            pltpu.VMEM(((height + HALO) * width, channels), BF16),
            pltpu.VMEM(((height + HALO) * width, channels), F32),
            pltpu.VMEM((height, width), F32),
            pltpu.VMEM((height, width), F32),
            pltpu.VMEM((height, width), F32),
            pltpu.VMEM((height, width), F32),
            pltpu.VMEM((height, width), F32),
            pltpu.VMEM((24, channels), F32),
            pltpu.VMEM((5, tp, width), F32),
            pltpu.VMEM((24, pixels), F32),
            pltpu.VMEM((2, padded, channels), F32),
            pltpu.VMEM((padded, channels), F32),
            pltpu.VMEM((part, channels), F32),
            pltpu.VMEM((groups, part, channels), jnp.int16),
            pltpu.VMEM((groups, part, channels), jnp.int16),
            pltpu.VMEM((2, groups, part, channels), jnp.int16),
            pltpu.VMEM((8, channels), F32),
            dma((tiles,)), dma((tiles,)), dma((tiles,)), dma((tiles,)),
            dma((4,)), dma((4,)), dma((4,)), dma((4,)),
            dma((CHUNKS + 1,)), dma((CHUNKS + 1,)), dma((groups,)), dma((groups,)),
            dma((groups,)), dma((groups,)), dma((groups,)), dma((groups,)),
        ],
        compiler_params=pltpu.CompilerParams(
            collective_id=0, has_side_effects=True, vmem_limit_bytes=58 * 1024 * 1024
        ),
        name="step",
    )(
        dest_tile.reshape(1, rows), pixel_bin, waves[0], target[0],
        conv_one.reshape(3, 3 * steps, channels), bias_one.reshape(1, channels), conv_two, bias_two.reshape(1, 1),
    )
    pred, one, bias, two = pl.pallas_call(
        finish_kernel,
        out_shape=(
            jax.ShapeDtypeStruct((height, width), F32),
            jax.ShapeDtypeStruct((3, 3, steps, channels), F32),
            jax.ShapeDtypeStruct((1, channels), F32),
            jax.ShapeDtypeStruct((3, 3, channels), F32),
        ),
        in_specs=[vmem] * 3,
        out_specs=(hbm,) * 4,
        scratch_shapes=[
            pltpu.VMEM((9, steps, channels), F32),
            pltpu.VMEM((1, channels), F32),
            pltpu.VMEM((3, 3, channels), F32),
            dma((12,)),
        ],
        name="finish",
    )(*[pltpu.with_memory_space_constraint(x, pltpu.VMEM) for x in held])
    return pred[None], one, bias[0], two


def solution(mesh):
    placed = (
        P("rep", "tile", None),
        P("rep", "tile", None),
        P("rep", "tile"),
        P("rep", "tile", None),
        P(),
        P(),
        P(),
        P(),
    )
    return jax.shard_map(
        functools.partial(on_device, mesh.shape["tile"], mesh.shape["rep"]),
        mesh=mesh,
        in_specs=placed,
        out_specs=(P("rep", "tile", None), P(), P(), P()),
        check_vma=False,
    )
```

```python
import functools

import jax
import jax.numpy as jnp
from jax import lax
from jax.experimental import pallas as pl
from jax.experimental.pallas import tpu as pltpu
from jax.sharding import PartitionSpec as P

CAP = 32
HALO = 4
CHUNKS = 4
LEVELS = 32000.0
MESH = pl.DeviceIdType.MESH
F32 = jnp.float32
BF16 = jnp.bfloat16


def iota(shape, dim):
    return lax.broadcasted_iota(jnp.int32, shape, dim)


def dot(a, b, dims=((1,), (0,))):
    return lax.dot_general(a, b, (dims, ((), ())), preferred_element_type=F32)


def repeat(count, body):
    if count <= 16:
        for n in range(count):
            body(n)
    else:

        def step(n, carry):
            body(n)
            return carry

        lax.fori_loop(0, count, step, 0)


def pair_rows(part):
    return 2 * part - 8


def small_row(n):
    return 8 * (n // 4) + (2 if n // 2 % 2 else 6) + n % 2


def exponent(largest):
    largest = jnp.maximum(jnp.max(largest, axis=0, keepdims=True), 2.0**-100)
    return jnp.ceil(jnp.log2(largest))


def encode(value, odd):
    last = value[-8:]
    row = iota(last.shape, 0)
    own = (row >= 4) == (odd == 1)
    inner = row - jnp.where(row >= 4, 4, 0)
    size = jnp.abs(last)
    largest = jnp.where(own, size, 0.0)
    for t in range(value.shape[0] // 8 - 1):
        largest = jnp.maximum(largest, jnp.abs(value[8 * t : 8 * t + 8]))
    one = exponent(largest)
    two = exponent(jnp.where(jnp.logical_or(own, inner < 2), 0.0, size))
    by_one = jnp.exp2(-one) * LEVELS
    by_two = jnp.exp2(-two) * LEVELS
    last = jnp.where(
        own, last * by_one, jnp.where(inner == 0, one, jnp.where(inner == 1, two, last * by_two))
    )
    if value.shape[0] > 8:
        last = jnp.concatenate([value[:-8] * by_one, last], axis=0)
    return jnp.round(last).astype(jnp.int32).astype(jnp.int16)


def decode(code, odd):
    value = code.astype(jnp.int32).astype(F32)
    last = value[-8:]
    own = (iota(last.shape, 0) >= 4) == (odd == 1)
    if isinstance(odd, int):
        one, two = (last[0:1], last[1:2]) if odd else (last[4:5], last[5:6])
    else:
        one = jnp.where(odd == 1, last[0:1], last[4:5])
        two = jnp.where(odd == 1, last[1:2], last[5:6])
    by_one = jnp.exp2(one) * (1.0 / LEVELS)
    last = last * jnp.where(own, by_one, jnp.exp2(two) * (1.0 / LEVELS))
    return jnp.concatenate([value[:-8] * by_one, last], axis=0) if value.shape[0] > 8 else last


def sum_shares(codes, odd):
    count = codes.shape[0]
    if count <= 16:
        out = decode(codes[0], odd)
        for s in range(1, count):
            out = out + decode(codes[s], odd)
        return out
    return lax.fori_loop(
        0, count, lambda s, out: out + decode(codes[s], odd), jnp.zeros(codes.shape[1:], F32)
    )


def holder(strip):
    pair, chip = strip // 4, strip // 2
    turned = 2 * pair + lax.rem(chip + pair, 2)
    return 2 * turned + lax.rem(strip, 2)


def step_kernel(
    tiles, reps, part,
    dest_hbm, bin_hbm, waves_hbm, target_hbm, w1_hbm, b1_hbm, w2_hbm, b2_hbm,
    pred_ref, raw_ref, extra_ref,
    dest_ref, bin_ref, waves_ref, target_ref, w1_ref, b1_ref, w2_ref, b2_ref, l_sem,
    sendw, sendb, recvw, recvb, grid, wide, pre_s, hid_s, acc_s, tlow, thigh, tmid, pout, pin, w2_s, taps, etap,
    full, pair, total, coded, recva, gathered, square,
    aw_send, aw_recv, ab_send, ab_recv, t_send, t_recv, g_send, g_recv,
    p_send, p_recv, s_send, s_recv, n_send, n_recv, f_send, f_recv,
):
    me = lax.axis_index("tile")
    rep = lax.axis_index("rep")
    rows, steps = waves_ref.shape
    height, width = target_ref.shape
    channels = b1_ref.shape[1]
    half = tiles // 2
    groups = half * reps
    core = lax.rem(me, 2)
    partner = me + 1 - 2 * core
    stride = half // 2 + 1
    chip = lax.rem(me // 2 * stride, half) * reps + rep
    strip = holder(me)
    chunks = CHUNKS
    pixels = height * width
    tall = height + HALO

    def tile_peer(k):
        return lax.rem(me + k, tiles)

    def group_peer(k):
        q = lax.rem(chip + k, groups)
        return q, device_at(q)

    def device_at(q):
        return {"tile": 2 * lax.rem(q // reps * stride, half) + core, "rep": lax.rem(q, reps)}

    loads = [
        pltpu.make_async_copy(src, dst, l_sem.at[k])
        for k, (src, dst) in enumerate(
            [
                (dest_hbm, dest_ref), (bin_hbm, bin_ref), (waves_hbm, waves_ref), (target_hbm, target_ref),
                (w1_hbm, w1_ref), (b1_hbm, b1_ref), (w2_hbm, w2_ref), (b2_hbm, b2_ref),
            ]
        )
    ]
    for load in loads:
        load.start()

    barrier = pltpu.get_barrier_semaphore()

    def greet(k, carry):
        pl.semaphore_signal(barrier, inc=1, device_id={"tile": tile_peer(k), "rep": rep}, device_id_type=MESH)
        return carry

    repeat(tiles - 1, lambda n: greet(n + 1, 0))

    def greet_far(k, carry):
        pl.semaphore_signal(
            barrier,
            inc=1,
            device_id={"tile": 2 * lax.rem(k, half) + core, "rep": lax.rem(rep + 1 + k // half, reps)},
            device_id_type=MESH,
        )
        return carry

    repeat((reps - 1) * half, lambda n: greet_far(n, 0))

    for load in loads[:4]:
        load.wait()

    hits = (iota((tiles, rows), 0) == dest_ref[...]).astype(F32)
    earlier = (iota((rows, rows), 0) < iota((rows, rows), 1)).astype(F32).astype(BF16)
    ranks = dot(hits.astype(BF16), earlier)
    rank = jnp.sum(hits * ranks, axis=0, keepdims=True)
    slot = jnp.sum(hits * (ranks + (CAP * iota((tiles, rows), 0)).astype(F32)), axis=0, keepdims=True)
    place = (iota((tiles * CAP, rows), 0).astype(F32) == slot).astype(F32).astype(BF16)
    sendw[...] = dot(place, waves_ref[...]).astype(BF16)
    lane = rank + (CAP * lax.rem(me, 4)).astype(F32)
    lanes = (iota((128, rows), 0).astype(F32) == lane).astype(F32).astype(BF16)
    bins = bin_ref[...]
    high = (bins // 32).astype(F32)
    low = (bins - 32 * (bins // 32)).astype(F32)
    named = 32.0 * dot((hits * high).astype(BF16), lanes, ((1,), (1,))) + dot(
        (hits * low).astype(BF16), lanes, ((1,), (1,))
    )
    for t in range(tiles):
        sendb[t] = named[t : t + 1, :]

    pl.semaphore_wait(barrier, tiles - 1 + (reps - 1) * half)

    def wave_copy(peer, source):
        return pltpu.make_async_remote_copy(
            src_ref=sendw.at[pl.ds(pl.multiple_of(holder(peer) * CAP, CAP), CAP)],
            dst_ref=recvw.at[pl.ds(pl.multiple_of(source * CAP, CAP), CAP)],
            send_sem=aw_send.at[peer],
            recv_sem=aw_recv.at[source],
            device_id={"tile": peer, "rep": rep},
            device_id_type=MESH,
        )

    def bin_copy(peer, source):
        return pltpu.make_async_remote_copy(
            src_ref=sendb.at[holder(peer)],
            dst_ref=recvb.at[source],
            send_sem=ab_send.at[peer],
            recv_sem=ab_recv.at[source],
            device_id={"tile": peer, "rep": rep},
            device_id_type=MESH,
        )

    def scatter(k, carry):
        peer = tile_peer(k)
        wave_copy(peer, me).start()
        bin_copy(peer, me).start()
        return carry

    lax.fori_loop(1, tiles, scatter, 0)

    def target_copy(peer, dst, k):
        return pltpu.make_async_remote_copy(
            src_ref=target_ref, dst_ref=dst, send_sem=t_send.at[k], recv_sem=t_recv.at[k],
            device_id={"tile": peer, "rep": rep}, device_id_type=MESH,
        )

    has_up = strip < tiles - 1
    has_down = strip > 0
    up = holder(jnp.minimum(strip + 1, tiles - 1))
    down = holder(jnp.maximum(strip - 1, 0))
    span = HALO * width
    step_px = 2 * width

    def halo_copy(peer, src, dst, k):
        return pltpu.make_async_remote_copy(
            src_ref=grid.at[pl.ds(src * width, step_px)], dst_ref=grid.at[pl.ds(dst * width, step_px)],
            send_sem=g_send.at[k], recv_sem=g_recv.at[k],
            device_id={"tile": peer, "rep": rep}, device_id_type=MESH,
        )

    to_up = target_copy(holder(jnp.minimum(me + 1, tiles - 1)), tlow, 0)
    to_down = target_copy(holder(jnp.maximum(me - 1, 0)), thigh, 1)
    to_mid = target_copy(strip, tmid, 2)
    grid_up = [halo_copy(up, height + 2, 2, 0), halo_copy(up, height, 0, 1)]
    grid_down = [halo_copy(down, HALO, height + HALO, 2), halo_copy(down, HALO + 2, height + HALO + 2, 3)]

    @pl.when(me < tiles - 1)
    def _():
        to_up.start()

    @pl.when(me > 0)
    def _():
        to_down.start()

    @pl.when(strip != me)
    def _():
        to_mid.start()

    @pl.when(strip == me)
    def _():
        tmid[...] = target_ref[...]

    @pl.when(jnp.logical_not(has_down))
    def _():
        grid[0:span, :] = jnp.zeros((span, steps), BF16)
        tlow[...] = jnp.zeros((height, width), F32)

    @pl.when(jnp.logical_not(has_up))
    def _():
        grid[span + pixels : span + pixels + span, :] = jnp.zeros((span, steps), BF16)
        thigh[...] = jnp.zeros((height, width), F32)

    own = pl.ds(pl.multiple_of(me * CAP, CAP), CAP)
    recvw[own, :] = sendw[pl.ds(pl.multiple_of(strip * CAP, CAP), CAP), :]
    recvb[me] = sendb[strip]
    for load in loads[4:]:
        load.wait()
    w2_s[...] = jnp.zeros(w2_s.shape, F32)
    for i in range(3):
        w2_s[8 * i : 8 * i + 3, :] = w2_ref[i].astype(F32)
    w2 = w2_s[...].astype(BF16)

    def arrive(k, carry):
        peer = tile_peer(k)
        wave_copy(peer, peer).wait_recv()
        bin_copy(peer, peer).wait_recv()
        return carry

    lax.fori_loop(1, tiles, arrive, 0)

    names = []
    for q in range(tiles // 4):
        names.append(recvb[4 * q] + recvb[4 * q + 1] + recvb[4 * q + 2] + recvb[4 * q + 3])
    names = jnp.concatenate(names, axis=1)
    stages = [(height - 2, has_up, grid_up[0]), (0, has_down, grid_down[0])]
    stages += [(height - 4, has_up, grid_up[1]), (2, has_down, grid_down[1])]
    stages += [(y, None, None) for y in range(HALO, height - HALO, 2)]
    for y, there, copy in stages:
        wanted = (iota((step_px, tiles * CAP), 0) + y * width).astype(F32)
        onehot = (wanted == names).astype(F32).astype(BF16)
        grid[span + y * width : span + y * width + step_px, :] = dot(onehot, recvw[...]).astype(BF16)
        if copy is not None:
            pl.when(there)(copy.start)

    column = iota((width, steps), 0)

    def spread(y):
        line = grid[y * width : (y + 1) * width, :]
        value = line.astype(F32)
        left = jnp.where(column >= 2, pltpu.roll(value, 2, 0), 0.0)
        right = jnp.where(column < width - 2, pltpu.roll(value, width - 2, 0), 0.0)
        wide[y * width : (y + 1) * width, 0:steps] = left.astype(BF16)
        wide[y * width : (y + 1) * width, steps : 2 * steps] = line
        wide[y * width : (y + 1) * width, 2 * steps : 3 * steps] = right.astype(BF16)

    for y in range(HALO, HALO + height):
        spread(y)

    bias = b1_ref[...]

    def convolve(y, terms, first, last):
        acc = jnp.zeros((step_px, channels), F32) + bias if first else acc_s[y * width : (y + 2) * width, :]
        for i in terms:
            acc = acc + dot(wide[(y + 2 * i) * width : (y + 2 * i + 2) * width, :], w1_ref[i])
        if not last:
            acc_s[y * width : (y + 2) * width, :] = acc
            return
        sig = 1.0 / (1.0 + jnp.exp(-acc))
        hidden = acc * sig
        if y < 2:
            hidden = jnp.where(has_down, hidden, 0.0)
        if y >= height + 2:
            hidden = jnp.where(has_up, hidden, 0.0)
        hid_s[y * width : (y + 2) * width, :] = hidden.astype(BF16)
        if 2 <= y < height + 2:
            pre_s[(y - 2) * width : y * width, :] = sig * (1.0 + acc * (1.0 - sig))

    begun = set()

    def advance(rows):
        for y in range(0, tall, 2):
            terms = [i for i in range(3) if y + 2 * i in rows]
            if terms:
                done[y] = done.get(y, 0) + len(terms)
                convolve(y, terms, y not in begun, done[y] == 3)
                begun.add(y)

    done = {}
    advance(range(HALO, HALO + height, 2))
    for k in range(2):

        @pl.when(has_down)
        def _():
            grid_up[k].wait_recv()

        @pl.when(has_up)
        def _():
            grid_down[k].wait_recv()

        fresh = [2 - 2 * k, height + HALO + 2 * k]
        for y in fresh:
            spread(y)
            spread(y + 1)
        advance(fresh)

    each = dot(w2, hid_s[...], ((1,), (1,)))
    span2 = (height + 2) * width
    summed = each[0:8, 0:span2] + each[8:16, width : width + span2] + each[16:24, 2 * width : 2 * width + span2]
    taps[...] = jnp.zeros(taps.shape, F32)
    for y in range(height + 2):
        for j in range(3):
            taps[j, y : y + 1, :] = summed[j : j + 1, y * width : (y + 1) * width]
    tp = taps.shape[1]
    x_at = iota((tp, width), 1)
    y_at = iota((tp, width), 0)
    pred = (
        b2_ref[...]
        + jnp.where(x_at >= 1, pltpu.roll(taps[0], 1, 1), 0.0)
        + taps[1]
        + jnp.where(x_at < width - 1, pltpu.roll(taps[2], width - 1, 1), 0.0)
    )

    @pl.when(has_down)
    def _():
        to_up.wait_recv()

    @pl.when(has_up)
    def _():
        to_down.wait_recv()

    @pl.when(strip != me)
    def _():
        to_mid.wait_recv()

    taps[3] = pred
    pout[...] = taps[3, 1 : 1 + height, :]
    hand_over = pltpu.make_async_remote_copy(
        src_ref=pout, dst_ref=pin, send_sem=t_send.at[3], recv_sem=t_recv.at[3],
        device_id={"tile": strip, "rep": rep}, device_id_type=MESH,
    )
    pl.when(strip != me)(hand_over.start)
    taps[4, 0:1, :] = tlow[height - 1 : height, :]
    taps[4, 1 : 1 + height, :] = tmid[...]
    taps[4, 1 + height : 2 + height, :] = thigh[0:1, :]
    inside = jnp.logical_and(
        jnp.logical_or(y_at >= 1, has_down),
        jnp.logical_and(y_at < height + 2, jnp.logical_or(y_at < height + 1, has_up)),
    )
    error = jnp.where(inside, (pred - taps[4]) / reps, 0.0).astype(BF16).astype(F32)
    taps[0] = jnp.where(x_at < width - 1, pltpu.roll(error, width - 1, 1), 0.0)
    taps[1] = error
    taps[2] = jnp.where(x_at >= 1, pltpu.roll(error, 1, 1), 0.0)
    etap[...] = jnp.zeros(etap.shape, F32)
    for i in range(3):
        for j in range(3):
            for y in range(height):
                etap[8 * i + j : 8 * i + j + 1, y * width : (y + 1) * width] = taps[j, y + 2 - i : y + 3 - i, :]
    errors = etap[...].astype(BF16)

    mine = hid_s[2 * width : 2 * width + pixels, :]
    grad_two = dot(errors, mine)
    back = dot(errors, w2, ((0,), (0,)))
    slope = (back * pre_s[...]).astype(BF16)
    grad_bias = dot(jnp.ones((8, pixels), BF16), slope)
    piece = steps // 2
    data = 9 * piece
    spare = pair_rows(part) * (groups // 2)
    for h in range(2):
        if spare > data:
            full[h, data:spare, :] = jnp.zeros((spare - data, channels), F32)
        full[h, spare:, :] = jnp.zeros((full.shape[1] - spare, channels), F32)
        for n in range(10):
            at = spare + small_row(n)
            full[h, at : at + 1, :] = grad_two[8 * (n // 3) + n % 3 :, :][0:1] if n < 9 else grad_bias[0:1]
    slab = spare // chunks

    def swap(a):
        rows_a = pl.ds(a * slab, slab) if a < chunks else pl.ds(spare, full.shape[1] - spare)
        return pltpu.make_async_remote_copy(
            src_ref=full.at[1 - core, rows_a], dst_ref=pair.at[rows_a],
            send_sem=p_send.at[a], recv_sem=p_recv.at[a],
            device_id={"tile": partner, "rep": rep}, device_id_type=MESH,
        )

    swap(chunks).start()
    started = 0
    for i in range(3):
        start = (2 + 2 * i) * width
        g = dot(wide[start : start + pixels, :], slope, ((0,), (0,)))
        for j in range(3):
            k = 3 * i + j
            for h in range(2):
                full[h, k * piece : (k + 1) * piece, :] = g[j * steps + h * piece : j * steps + (h + 1) * piece, :]
        while started < chunks and ((started + 1) * slab <= 3 * (i + 1) * piece or i == 2):
            swap(started).start()
            started += 1

    def share_copy(q, source):
        return pltpu.make_async_remote_copy(
            src_ref=coded.at[q], dst_ref=recva.at[source],
            send_sem=s_send.at[q], recv_sem=s_recv.at[source],
            device_id=device_at(q), device_id_type=MESH,
        )

    whole = part - 8
    per_pair = pair_rows(part)
    top = iota((8, channels), 0) < 4

    def hand_out(p):
        rows_p = pl.ds(p * per_pair, per_pair)
        rows_s = pl.ds(spare + p * 8, 8)
        x = full[core, rows_p, :] + pair[rows_p, :]
        extra = full[core, rows_s, :] + pair[rows_s, :]
        for odd in range(2):
            q = 2 * p + odd
            mixed = x[whole : whole + 8]
            mixed = jnp.where(top, extra, mixed) if odd else jnp.where(top, mixed, extra)
            value = x[whole + 8 :] if odd else x[:whole]
            value = jnp.concatenate([value, mixed], axis=0) if whole else mixed

            @pl.when(chip == q)
            def _():
                total[...] = value

            @pl.when(chip != q)
            def _():
                coded[q] = encode(value, odd)
                share_copy(q, chip).start()

    swap(chunks).wait_recv()
    pairs_each = groups // 2 // chunks
    for a in range(chunks):
        swap(a).wait_recv()
        repeat(pairs_each, lambda n: hand_out(a * pairs_each + n))

    def arrived(k):
        share_copy(lax.rem(chip + k, groups), lax.rem(chip + groups - k, groups)).wait_recv()

    repeat(groups - 1, lambda n: arrived(n + 1))
    parity = lax.rem(chip, 2)
    recva[chip] = jnp.zeros(recva.shape[1:], recva.dtype)
    total[...] = total[...] + sum_shares(recva, parity)
    gathered[core, chip] = encode(total[...], parity)

    def spread_copy(device, source):
        return pltpu.make_async_remote_copy(
            src_ref=gathered.at[core, chip], dst_ref=gathered.at[core, source],
            send_sem=n_send.at[source], recv_sem=n_recv.at[source], device_id=device, device_id_type=MESH,
        )

    def spread_to(q):
        @pl.when(chip != q)
        def _():
            pltpu.make_async_remote_copy(
                src_ref=gathered.at[core, chip], dst_ref=gathered.at[core, chip],
                send_sem=n_send.at[q], recv_sem=n_recv.at[chip], device_id=device_at(q), device_id_type=MESH,
            ).start()

    repeat(groups, spread_to)

    def forward(q, which):
        return pltpu.make_async_remote_copy(
            src_ref=gathered.at[which, q], dst_ref=gathered.at[which, q],
            send_sem=f_send.at[q], recv_sem=f_recv.at[q],
            device_id={"tile": partner, "rep": rep}, device_id_type=MESH,
        )

    forward(chip, core).start()

    @pl.when(strip == me)
    def _():
        pred_ref[...] = pout[...]

    @pl.when(strip != me)
    def _():
        to_mid.wait_send()
        hand_over.wait()
        pred_ref[...] = pin[...]

    @pl.when(me < tiles - 1)
    def _():
        to_up.wait_send()

    @pl.when(me > 0)
    def _():
        to_down.wait_send()

    @pl.when(has_up)
    def _():
        for copy in grid_up:
            copy.wait_send()

    @pl.when(has_down)
    def _():
        for copy in grid_down:
            copy.wait_send()

    def sent(k, carry):
        peer = tile_peer(k)
        wave_copy(peer, me).wait_send()
        bin_copy(peer, me).wait_send()
        return carry

    lax.fori_loop(1, tiles, sent, 0)
    for a in range(chunks + 1):
        swap(a).wait_send()

    def handed(k):
        share_copy(lax.rem(chip + k, groups), chip).wait_send()

    repeat(groups - 1, lambda n: handed(n + 1))

    square[...] = jnp.zeros(square.shape, F32)
    count = 9 * piece

    def keep(h, p):
        even = decode(gathered[h, 2 * p], 0)
        odd = decode(gathered[h, 2 * p + 1], 1)
        tiles = [even[8 * t : 8 * t + 8] for t in range(whole // 8)]
        tiles.append(jnp.where(top, even[whole:], odd[whole:]))
        tiles += [odd[8 * t : 8 * t + 8] for t in range(whole // 8)]
        total_sq = square[h]
        for t, tile in enumerate(tiles):
            at = p * per_pair + 8 * t
            k, r = at // piece, at % piece
            raw_ref[k, pl.ds(pl.multiple_of(h * piece + r, 8), 8), :] = tile
            total_sq = total_sq + tile * tile
        square[h] = total_sq

    def keep_pair(h, p):
        if isinstance(p, int):
            if p * per_pair < count:
                keep(h, p)
        else:
            pl.when(p * per_pair < count)(lambda: keep(h, p))

    def take(p):
        for q in (2 * p, 2 * p + 1):

            @pl.when(chip != q)
            def _():
                spread_copy(device_at(q), q).wait_recv()
                forward(q, core).start()

        keep_pair(core, p)

    repeat(groups // 2, take)

    def shared(k, carry):
        q, device = group_peer(k)
        spread_copy(device, q).wait_send()
        return carry

    repeat(groups - 1, lambda n: shared(n + 1, 0))

    def fetch(p):
        for q in (2 * p, 2 * p + 1):
            forward(q, 1 - core).wait_recv()
        keep_pair(1 - core, p)

    repeat(groups // 2, fetch)
    extra_ref[10:16, :] = jnp.zeros((6, channels), F32) + 1.0 / jnp.sqrt(
        jnp.sum(square[0] + square[1]) / (9 * steps * channels) + 1e-06
    )
    smalls = []
    for p in range(3):
        smalls.append(jnp.where(top, decode(gathered[0, 2 * p + 1], 1)[whole:], decode(gathered[0, 2 * p], 0)[whole:]))
    rows = []
    for n in range(10):
        at = small_row(n)
        rows.append(smalls[at // 8][at % 8 : at % 8 + 1])
    two = jnp.zeros((1, channels), F32)
    for row in rows[:9]:
        two = two + row * row
    scale_two = 1.0 / jnp.sqrt(jnp.sum(two) / (9 * channels) + 1e-06)
    for n in range(9):
        extra_ref[n : n + 1, :] = rows[n] * scale_two
    extra_ref[9:10, :] = rows[9] / jnp.sqrt(jnp.sum(rows[9] * rows[9]) / channels + 1e-06)

    def passed(q, carry):
        forward(q, core).wait_send()
        return carry

    repeat(groups, lambda q: passed(q, 0))


def finish_kernel(pred_ref, raw_ref, extra_ref, pred_out, u1_out, ub_out, u2_out, u1, ub, u2, sem):
    ub[...] = extra_ref[9:10, :]
    for n in range(9):
        u2[n // 3, n % 3 : n % 3 + 1, :] = extra_ref[n : n + 1, :]
    copies = [
        pltpu.make_async_copy(src, dst, sem.at[k])
        for k, (src, dst) in enumerate([(pred_ref, pred_out), (ub, ub_out), (u2, u2_out)])
    ]
    for copy in copies:
        copy.start()
    scale = extra_ref[10:11, :]
    for k in range(9):
        u1[k] = raw_ref[k] * scale
        copies.append(pltpu.make_async_copy(u1.at[k], u1_out.at[k // 3, k % 3], sem.at[3 + k]))
        copies[-1].start()
    for copy in copies:
        copy.wait()


def on_device(tiles, reps, waves, dest_tile, pixel_bin, target, conv_one, bias_one, conv_two, bias_two):
    rows, steps = waves.shape[1:]
    height, width = target.shape[1:]
    channels = conv_one.shape[3]
    pixels = height * width
    groups = tiles // 2 * reps
    units = -(-9 * (steps // 8) // groups) // 2 * 2 + 1
    part = 4 * units + 4
    padded = (pair_rows(part) + 8) * (groups // 2)
    hbm = pl.BlockSpec(memory_space=pltpu.HBM)
    tp = -(-(height + 2) // 8) * 8
    dma = pltpu.SemaphoreType.DMA
    vmem = pl.BlockSpec(memory_space=pltpu.VMEM)
    held = pl.pallas_call(
        functools.partial(step_kernel, tiles, reps, part),
        out_shape=(
            pltpu.VMEM((height, width), F32),
            pltpu.VMEM((9, steps, channels), F32),
            pltpu.VMEM((16, channels), F32),
        ),
        in_specs=[hbm] * 8,
        out_specs=(vmem,) * 3,
        scratch_shapes=[
            pltpu.VMEM((1, rows), jnp.int32),
            pltpu.VMEM((1, rows), jnp.int32),
            pltpu.VMEM((rows, steps), BF16),
            pltpu.VMEM((height, width), F32),
            pltpu.VMEM((3, 3 * steps, channels), BF16),
            pltpu.VMEM((1, channels), F32),
            pltpu.VMEM((3, 3, channels), BF16),
            pltpu.VMEM((1, 1), F32),
            dma((8,)),
            pltpu.VMEM((tiles * CAP, steps), BF16),
            pltpu.VMEM((tiles, 1, 128), F32),
            pltpu.VMEM((tiles * CAP, steps), BF16),
            pltpu.VMEM((tiles, 1, 128), F32),
            pltpu.VMEM(((height + 2 * HALO) * width, steps), BF16),
            pltpu.VMEM(((height + 2 * HALO) * width, 3 * steps), BF16),
            pltpu.VMEM((pixels, channels), F32),
            pltpu.VMEM(((height + HALO) * width, channels), BF16),
            pltpu.VMEM(((height + HALO) * width, channels), F32),
            pltpu.VMEM((height, width), F32),
            pltpu.VMEM((height, width), F32),
            pltpu.VMEM((height, width), F32),
            pltpu.VMEM((height, width), F32),
            pltpu.VMEM((height, width), F32),
            pltpu.VMEM((24, channels), F32),
            pltpu.VMEM((5, tp, width), F32),
            pltpu.VMEM((24, pixels), F32),
            pltpu.VMEM((2, padded, channels), F32),
            pltpu.VMEM((padded, channels), F32),
            pltpu.VMEM((part, channels), F32),
            pltpu.VMEM((groups, part, channels), jnp.int16),
            pltpu.VMEM((groups, part, channels), jnp.int16),
            pltpu.VMEM((2, groups, part, channels), jnp.int16),
            pltpu.VMEM((2, 8, channels), F32),
            dma((tiles,)), dma((tiles,)), dma((tiles,)), dma((tiles,)),
            dma((4,)), dma((4,)), dma((4,)), dma((4,)),
            dma((CHUNKS + 1,)), dma((CHUNKS + 1,)), dma((groups,)), dma((groups,)),
            dma((groups,)), dma((groups,)), dma((groups,)), dma((groups,)),
        ],
        compiler_params=pltpu.CompilerParams(
            collective_id=0, has_side_effects=True, vmem_limit_bytes=58 * 1024 * 1024
        ),
        name="step",
    )(
        dest_tile.reshape(1, rows), pixel_bin, waves[0], target[0],
        conv_one.reshape(3, 3 * steps, channels), bias_one.reshape(1, channels), conv_two, bias_two.reshape(1, 1),
    )
    pred, one, bias, two = pl.pallas_call(
        finish_kernel,
        out_shape=(
            jax.ShapeDtypeStruct((height, width), F32),
            jax.ShapeDtypeStruct((3, 3, steps, channels), F32),
            jax.ShapeDtypeStruct((1, channels), F32),
            jax.ShapeDtypeStruct((3, 3, channels), F32),
        ),
        in_specs=[vmem] * 3,
        out_specs=(hbm,) * 4,
        scratch_shapes=[
            pltpu.VMEM((9, steps, channels), F32),
            pltpu.VMEM((1, channels), F32),
            pltpu.VMEM((3, 3, channels), F32),
            dma((12,)),
        ],
        name="finish",
    )(*[pltpu.with_memory_space_constraint(x, pltpu.VMEM) for x in held])
    return pred[None], one, bias[0], two


def solution(mesh):
    placed = (
        P("rep", "tile", None),
        P("rep", "tile", None),
        P("rep", "tile"),
        P("rep", "tile", None),
        P(),
        P(),
        P(),
        P(),
    )
    return jax.shard_map(
        functools.partial(on_device, mesh.shape["tile"], mesh.shape["rep"]),
        mesh=mesh,
        in_specs=placed,
        out_specs=(P("rep", "tile", None), P(), P(), P()),
        check_vma=False,
    )
```

```python
import functools

import jax
import jax.numpy as jnp
from jax import lax
from jax.experimental import pallas as pl
from jax.experimental.pallas import tpu as pltpu
from jax.sharding import PartitionSpec as P

CAP = 32
HALO = 4
CHUNKS = 4
LEVELS = 32000.0
MESH = pl.DeviceIdType.MESH
F32 = jnp.float32
BF16 = jnp.bfloat16


def iota(shape, dim):
    return lax.broadcasted_iota(jnp.int32, shape, dim)


def dot(a, b, dims=((1,), (0,))):
    return lax.dot_general(a, b, (dims, ((), ())), preferred_element_type=F32)


def repeat(count, body):
    if count <= 16:
        for n in range(count):
            body(n)
    else:

        def step(n, carry):
            body(n)
            return carry

        lax.fori_loop(0, count, step, 0)


def pair_rows(part):
    return 2 * part - 8


def small_row(n):
    return 8 * (n // 4) + (2 if n // 2 % 2 else 6) + n % 2


def exponent(largest):
    largest = jnp.maximum(jnp.max(largest, axis=0, keepdims=True), 2.0**-100)
    return jnp.ceil(jnp.log2(largest))


def encode(value, odd):
    last = value[-8:]
    row = iota(last.shape, 0)
    own = (row >= 4) == (odd == 1)
    inner = row - jnp.where(row >= 4, 4, 0)
    size = jnp.abs(last)
    largest = jnp.where(own, size, 0.0)
    for t in range(value.shape[0] // 8 - 1):
        largest = jnp.maximum(largest, jnp.abs(value[8 * t : 8 * t + 8]))
    one = exponent(largest)
    two = exponent(jnp.where(jnp.logical_or(own, inner < 2), 0.0, size))
    by_one = jnp.exp2(-one) * LEVELS
    by_two = jnp.exp2(-two) * LEVELS
    last = jnp.where(
        own, last * by_one, jnp.where(inner == 0, one, jnp.where(inner == 1, two, last * by_two))
    )
    if value.shape[0] > 8:
        last = jnp.concatenate([value[:-8] * by_one, last], axis=0)
    return jnp.round(last).astype(jnp.int32).astype(jnp.int16)


def decode(code, odd):
    value = code.astype(jnp.int32).astype(F32)
    last = value[-8:]
    own = (iota(last.shape, 0) >= 4) == (odd == 1)
    if isinstance(odd, int):
        one, two = (last[0:1], last[1:2]) if odd else (last[4:5], last[5:6])
    else:
        one = jnp.where(odd == 1, last[0:1], last[4:5])
        two = jnp.where(odd == 1, last[1:2], last[5:6])
    by_one = jnp.exp2(one) * (1.0 / LEVELS)
    last = last * jnp.where(own, by_one, jnp.exp2(two) * (1.0 / LEVELS))
    return jnp.concatenate([value[:-8] * by_one, last], axis=0) if value.shape[0] > 8 else last


def sum_shares(codes, odd):
    count = codes.shape[0]
    if count <= 16:
        out = decode(codes[0], odd)
        for s in range(1, count):
            out = out + decode(codes[s], odd)
        return out
    return lax.fori_loop(
        0, count, lambda s, out: out + decode(codes[s], odd), jnp.zeros(codes.shape[1:], F32)
    )


def holder(strip):
    pair, chip = strip // 4, strip // 2
    turned = 2 * pair + lax.rem(chip + pair, 2)
    return 2 * turned + lax.rem(strip, 2)


def step_kernel(
    tiles, reps, part,
    dest_hbm, bin_hbm, waves_hbm, target_hbm, w1_hbm, b1_hbm, w2_hbm, b2_hbm,
    pred_ref, raw_ref, extra_ref,
    dest_ref, bin_ref, waves_ref, target_ref, w1_ref, b1_ref, w2_ref, b2_ref, l_sem,
    sendw, sendb, recvw, recvb, grid, wide, pre_s, hid_s, acc_s, tlow, thigh, tmid, pout, pin, w2_s, taps, etap,
    full, pair, total, coded, recva, gathered, square,
    aw_send, aw_recv, ab_send, ab_recv, t_send, t_recv, g_send, g_recv,
    p_send, p_recv, s_send, s_recv, n_send, n_recv, f_send, f_recv,
):
    me = lax.axis_index("tile")
    rep = lax.axis_index("rep")
    rows, steps = waves_ref.shape
    height, width = target_ref.shape
    channels = b1_ref.shape[1]
    half = tiles // 2
    groups = half * reps
    core = lax.rem(me, 2)
    partner = me + 1 - 2 * core
    stride = half // 2 + 1
    chip = lax.rem(me // 2 * stride, half) * reps + rep
    strip = holder(me)
    chunks = CHUNKS
    pixels = height * width
    tall = height + HALO

    def tile_peer(k):
        return lax.rem(me + k, tiles)

    def group_peer(k):
        q = lax.rem(chip + k, groups)
        return q, device_at(q)

    def device_at(q):
        return {"tile": 2 * lax.rem(q // reps * stride, half) + core, "rep": lax.rem(q, reps)}

    loads = [
        pltpu.make_async_copy(src, dst, l_sem.at[k])
        for k, (src, dst) in enumerate(
            [
                (dest_hbm, dest_ref), (bin_hbm, bin_ref), (waves_hbm, waves_ref), (target_hbm, target_ref),
                (w1_hbm, w1_ref), (b1_hbm, b1_ref), (w2_hbm, w2_ref), (b2_hbm, b2_ref),
            ]
        )
    ]
    for load in loads:
        load.start()

    barrier = pltpu.get_barrier_semaphore()

    def greet(k, carry):
        pl.semaphore_signal(barrier, inc=1, device_id={"tile": tile_peer(k), "rep": rep}, device_id_type=MESH)
        return carry

    repeat(tiles - 1, lambda n: greet(n + 1, 0))

    def greet_far(k, carry):
        pl.semaphore_signal(
            barrier,
            inc=1,
            device_id={"tile": 2 * lax.rem(k, half) + core, "rep": lax.rem(rep + 1 + k // half, reps)},
            device_id_type=MESH,
        )
        return carry

    repeat((reps - 1) * half, lambda n: greet_far(n, 0))

    for load in loads[:4]:
        load.wait()

    hits = (iota((tiles, rows), 0) == dest_ref[...]).astype(F32)
    earlier = (iota((rows, rows), 0) < iota((rows, rows), 1)).astype(F32).astype(BF16)
    ranks = dot(hits.astype(BF16), earlier)
    rank = jnp.sum(hits * ranks, axis=0, keepdims=True)
    slot = jnp.sum(hits * (ranks + (CAP * iota((tiles, rows), 0)).astype(F32)), axis=0, keepdims=True)
    place = (iota((tiles * CAP, rows), 0).astype(F32) == slot).astype(F32).astype(BF16)
    sendw[...] = dot(place, waves_ref[...]).astype(BF16)
    lane = rank + (CAP * lax.rem(me, 4)).astype(F32)
    lanes = (iota((128, rows), 0).astype(F32) == lane).astype(F32).astype(BF16)
    bins = bin_ref[...]
    high = (bins // 32).astype(F32)
    low = (bins - 32 * (bins // 32)).astype(F32)
    named = 32.0 * dot((hits * high).astype(BF16), lanes, ((1,), (1,))) + dot(
        (hits * low).astype(BF16), lanes, ((1,), (1,))
    )
    for t in range(tiles):
        sendb[t] = named[t : t + 1, :]

    pl.semaphore_wait(barrier, tiles - 1 + (reps - 1) * half)

    def wave_copy(peer, source):
        return pltpu.make_async_remote_copy(
            src_ref=sendw.at[pl.ds(pl.multiple_of(holder(peer) * CAP, CAP), CAP)],
            dst_ref=recvw.at[pl.ds(pl.multiple_of(source * CAP, CAP), CAP)],
            send_sem=aw_send.at[peer],
            recv_sem=aw_recv.at[source],
            device_id={"tile": peer, "rep": rep},
            device_id_type=MESH,
        )

    def bin_copy(peer, source):
        return pltpu.make_async_remote_copy(
            src_ref=sendb.at[holder(peer)],
            dst_ref=recvb.at[source],
            send_sem=ab_send.at[peer],
            recv_sem=ab_recv.at[source],
            device_id={"tile": peer, "rep": rep},
            device_id_type=MESH,
        )

    def scatter(k, carry):
        peer = tile_peer(k)
        wave_copy(peer, me).start()
        bin_copy(peer, me).start()
        return carry

    lax.fori_loop(1, tiles, scatter, 0)

    def target_copy(peer, dst, k):
        return pltpu.make_async_remote_copy(
            src_ref=target_ref, dst_ref=dst, send_sem=t_send.at[k], recv_sem=t_recv.at[k],
            device_id={"tile": peer, "rep": rep}, device_id_type=MESH,
        )

    has_up = strip < tiles - 1
    has_down = strip > 0
    up = holder(jnp.minimum(strip + 1, tiles - 1))
    down = holder(jnp.maximum(strip - 1, 0))
    span = HALO * width
    step_px = 2 * width

    def halo_copy(peer, src, dst, k):
        return pltpu.make_async_remote_copy(
            src_ref=grid.at[pl.ds(src * width, step_px)], dst_ref=grid.at[pl.ds(dst * width, step_px)],
            send_sem=g_send.at[k], recv_sem=g_recv.at[k],
            device_id={"tile": peer, "rep": rep}, device_id_type=MESH,
        )

    to_up = target_copy(holder(jnp.minimum(me + 1, tiles - 1)), tlow, 0)
    to_down = target_copy(holder(jnp.maximum(me - 1, 0)), thigh, 1)
    to_mid = target_copy(strip, tmid, 2)
    grid_up = [halo_copy(up, height + 2, 2, 0), halo_copy(up, height, 0, 1)]
    grid_down = [halo_copy(down, HALO, height + HALO, 2), halo_copy(down, HALO + 2, height + HALO + 2, 3)]

    @pl.when(me < tiles - 1)
    def _():
        to_up.start()

    @pl.when(me > 0)
    def _():
        to_down.start()

    @pl.when(strip != me)
    def _():
        to_mid.start()

    @pl.when(strip == me)
    def _():
        tmid[...] = target_ref[...]

    @pl.when(jnp.logical_not(has_down))
    def _():
        grid[0:span, :] = jnp.zeros((span, steps), BF16)
        tlow[...] = jnp.zeros((height, width), F32)

    @pl.when(jnp.logical_not(has_up))
    def _():
        grid[span + pixels : span + pixels + span, :] = jnp.zeros((span, steps), BF16)
        thigh[...] = jnp.zeros((height, width), F32)

    own = pl.ds(pl.multiple_of(me * CAP, CAP), CAP)
    recvw[own, :] = sendw[pl.ds(pl.multiple_of(strip * CAP, CAP), CAP), :]
    recvb[me] = sendb[strip]
    for load in loads[4:]:
        load.wait()
    w2_s[...] = jnp.zeros(w2_s.shape, F32)
    for i in range(3):
        w2_s[8 * i : 8 * i + 3, :] = w2_ref[i].astype(F32)
    w2 = w2_s[...].astype(BF16)

    def arrive(k, carry):
        peer = tile_peer(k)
        wave_copy(peer, peer).wait_recv()
        bin_copy(peer, peer).wait_recv()
        return carry

    lax.fori_loop(1, tiles, arrive, 0)

    names = []
    for q in range(tiles // 4):
        names.append(recvb[4 * q] + recvb[4 * q + 1] + recvb[4 * q + 2] + recvb[4 * q + 3])
    names = jnp.concatenate(names, axis=1)
    stages = [(height - 2, has_up, grid_up[0]), (0, has_down, grid_down[0])]
    stages += [(height - 4, has_up, grid_up[1]), (2, has_down, grid_down[1])]
    stages += [(y, None, None) for y in range(HALO, height - HALO, 2)]
    for y, there, copy in stages:
        wanted = (iota((step_px, tiles * CAP), 0) + y * width).astype(F32)
        onehot = (wanted == names).astype(F32).astype(BF16)
        grid[span + y * width : span + y * width + step_px, :] = dot(onehot, recvw[...]).astype(BF16)
        if copy is not None:
            pl.when(there)(copy.start)

    column = iota((width, steps), 0)

    def spread(y):
        line = grid[y * width : (y + 1) * width, :]
        value = line.astype(F32)
        left = jnp.where(column >= 2, pltpu.roll(value, 2, 0), 0.0)
        right = jnp.where(column < width - 2, pltpu.roll(value, width - 2, 0), 0.0)
        wide[y * width : (y + 1) * width, 0:steps] = left.astype(BF16)
        wide[y * width : (y + 1) * width, steps : 2 * steps] = line
        wide[y * width : (y + 1) * width, 2 * steps : 3 * steps] = right.astype(BF16)

    for y in range(HALO, HALO + height):
        spread(y)

    bias = b1_ref[...]

    def convolve(y, terms, first, last):
        acc = jnp.zeros((step_px, channels), F32) + bias if first else acc_s[y * width : (y + 2) * width, :]
        for i in terms:
            acc = acc + dot(wide[(y + 2 * i) * width : (y + 2 * i + 2) * width, :], w1_ref[i])
        if not last:
            acc_s[y * width : (y + 2) * width, :] = acc
            return
        sig = 1.0 / (1.0 + jnp.exp(-acc))
        hidden = acc * sig
        if y < 2:
            hidden = jnp.where(has_down, hidden, 0.0)
        if y >= height + 2:
            hidden = jnp.where(has_up, hidden, 0.0)
        hid_s[y * width : (y + 2) * width, :] = hidden.astype(BF16)
        if 2 <= y < height + 2:
            pre_s[(y - 2) * width : y * width, :] = sig * (1.0 + acc * (1.0 - sig))

    begun = set()

    def advance(rows):
        for y in range(0, tall, 2):
            terms = [i for i in range(3) if y + 2 * i in rows]
            if terms:
                done[y] = done.get(y, 0) + len(terms)
                convolve(y, terms, y not in begun, done[y] == 3)
                begun.add(y)

    done = {}
    advance(range(HALO, HALO + height, 2))
    for k in range(2):

        @pl.when(has_down)
        def _():
            grid_up[k].wait_recv()

        @pl.when(has_up)
        def _():
            grid_down[k].wait_recv()

        fresh = [2 - 2 * k, height + HALO + 2 * k]
        for y in fresh:
            spread(y)
            spread(y + 1)
        advance(fresh)

    each = dot(w2, hid_s[...], ((1,), (1,)))
    span2 = (height + 2) * width
    summed = each[0:8, 0:span2] + each[8:16, width : width + span2] + each[16:24, 2 * width : 2 * width + span2]
    taps[...] = jnp.zeros(taps.shape, F32)
    for y in range(height + 2):
        for j in range(3):
            taps[j, y : y + 1, :] = summed[j : j + 1, y * width : (y + 1) * width]
    tp = taps.shape[1]
    x_at = iota((tp, width), 1)
    y_at = iota((tp, width), 0)
    pred = (
        b2_ref[...]
        + jnp.where(x_at >= 1, pltpu.roll(taps[0], 1, 1), 0.0)
        + taps[1]
        + jnp.where(x_at < width - 1, pltpu.roll(taps[2], width - 1, 1), 0.0)
    )

    @pl.when(has_down)
    def _():
        to_up.wait_recv()

    @pl.when(has_up)
    def _():
        to_down.wait_recv()

    @pl.when(strip != me)
    def _():
        to_mid.wait_recv()

    taps[3] = pred
    pout[...] = taps[3, 1 : 1 + height, :]
    hand_over = pltpu.make_async_remote_copy(
        src_ref=pout, dst_ref=pin, send_sem=t_send.at[3], recv_sem=t_recv.at[3],
        device_id={"tile": strip, "rep": rep}, device_id_type=MESH,
    )
    pl.when(strip != me)(hand_over.start)
    taps[4, 0:1, :] = tlow[height - 1 : height, :]
    taps[4, 1 : 1 + height, :] = tmid[...]
    taps[4, 1 + height : 2 + height, :] = thigh[0:1, :]
    inside = jnp.logical_and(
        jnp.logical_or(y_at >= 1, has_down),
        jnp.logical_and(y_at < height + 2, jnp.logical_or(y_at < height + 1, has_up)),
    )
    error = jnp.where(inside, (pred - taps[4]) / reps, 0.0).astype(BF16).astype(F32)
    taps[0] = jnp.where(x_at < width - 1, pltpu.roll(error, width - 1, 1), 0.0)
    taps[1] = error
    taps[2] = jnp.where(x_at >= 1, pltpu.roll(error, 1, 1), 0.0)
    etap[...] = jnp.zeros(etap.shape, F32)
    for i in range(3):
        for j in range(3):
            for y in range(height):
                etap[8 * i + j : 8 * i + j + 1, y * width : (y + 1) * width] = taps[j, y + 2 - i : y + 3 - i, :]
    errors = etap[...].astype(BF16)

    mine = hid_s[2 * width : 2 * width + pixels, :]
    grad_two = dot(errors, mine)
    back = dot(errors, w2, ((0,), (0,)))
    slope = (back * pre_s[...]).astype(BF16)
    grad_bias = dot(jnp.ones((8, pixels), BF16), slope)
    piece = steps // 2
    data = 9 * piece
    spare = pair_rows(part) * (groups // 2)
    for h in range(2):
        if spare > data:
            full[h, data:spare, :] = jnp.zeros((spare - data, channels), F32)
        full[h, spare:, :] = jnp.zeros((full.shape[1] - spare, channels), F32)
        for n in range(10):
            at = spare + small_row(n)
            full[h, at : at + 1, :] = grad_two[8 * (n // 3) + n % 3 :, :][0:1] if n < 9 else grad_bias[0:1]
    slab = spare // chunks

    def swap(a):
        rows_a = pl.ds(a * slab, slab) if a < chunks else pl.ds(spare, full.shape[1] - spare)
        return pltpu.make_async_remote_copy(
            src_ref=full.at[1 - core, rows_a], dst_ref=pair.at[rows_a],
            send_sem=p_send.at[a], recv_sem=p_recv.at[a],
            device_id={"tile": partner, "rep": rep}, device_id_type=MESH,
        )

    swap(chunks).start()
    first_rows = data - 3 * steps

    def grads(h, late):
        if h == 0:
            i, lanes, skip, at, size = (1, slice(0, 2 * steps), 0, 3 * steps, first_rows) if late else (
                0, slice(0, 3 * steps), 0, 0, 3 * steps)
        else:
            i, lanes, skip, at, size = (2, slice(0, 3 * steps), 0, first_rows, 3 * steps) if late else (
                1, slice(steps, 3 * steps), 2 * steps - first_rows, 0, first_rows)
        start = (2 + 2 * i) * width
        g = dot(wide[start : start + pixels, lanes], slope, ((0,), (0,)))
        full[h, at : at + size, :] = g[skip : skip + size]
        return at + size

    for which in range(2):

        @pl.when(core == which)
        def _():
            started = 0
            for late in (False, True):
                ready = grads(1 - which, late)
                while started < chunks and ((started + 1) * slab <= ready or late):
                    swap(started).start()
                    started += 1
            for late in (False, True):
                grads(which, late)

    def share_copy(q, source):
        return pltpu.make_async_remote_copy(
            src_ref=coded.at[q], dst_ref=recva.at[source],
            send_sem=s_send.at[q], recv_sem=s_recv.at[source],
            device_id=device_at(q), device_id_type=MESH,
        )

    whole = part - 8
    per_pair = pair_rows(part)
    top = iota((8, channels), 0) < 4

    def hand_out(p):
        rows_p = pl.ds(p * per_pair, per_pair)
        rows_s = pl.ds(spare + p * 8, 8)
        x = full[core, rows_p, :] + pair[rows_p, :]
        extra = full[core, rows_s, :] + pair[rows_s, :]
        for odd in range(2):
            q = 2 * p + odd
            mixed = x[whole : whole + 8]
            mixed = jnp.where(top, extra, mixed) if odd else jnp.where(top, mixed, extra)
            value = x[whole + 8 :] if odd else x[:whole]
            value = jnp.concatenate([value, mixed], axis=0) if whole else mixed

            @pl.when(chip == q)
            def _():
                total[...] = value

            @pl.when(chip != q)
            def _():
                coded[q] = encode(value, odd)
                share_copy(q, chip).start()

    swap(chunks).wait_recv()
    pairs_each = groups // 2 // chunks
    for a in range(chunks):
        swap(a).wait_recv()
        repeat(pairs_each, lambda n: hand_out(a * pairs_each + n))

    def arrived(k):
        share_copy(lax.rem(chip + k, groups), lax.rem(chip + groups - k, groups)).wait_recv()

    repeat(groups - 1, lambda n: arrived(n + 1))
    parity = lax.rem(chip, 2)
    recva[chip] = jnp.zeros(recva.shape[1:], recva.dtype)
    total[...] = total[...] + sum_shares(recva, parity)
    gathered[core, chip] = encode(total[...], parity)

    def spread_copy(device, source):
        return pltpu.make_async_remote_copy(
            src_ref=gathered.at[core, chip], dst_ref=gathered.at[core, source],
            send_sem=n_send.at[source], recv_sem=n_recv.at[source], device_id=device, device_id_type=MESH,
        )

    def spread_to(q):
        @pl.when(chip != q)
        def _():
            pltpu.make_async_remote_copy(
                src_ref=gathered.at[core, chip], dst_ref=gathered.at[core, chip],
                send_sem=n_send.at[q], recv_sem=n_recv.at[chip], device_id=device_at(q), device_id_type=MESH,
            ).start()

    repeat(groups, spread_to)

    def forward(q, which):
        return pltpu.make_async_remote_copy(
            src_ref=gathered.at[which, q], dst_ref=gathered.at[which, q],
            send_sem=f_send.at[q], recv_sem=f_recv.at[q],
            device_id={"tile": partner, "rep": rep}, device_id_type=MESH,
        )

    forward(chip, core).start()

    @pl.when(strip == me)
    def _():
        pred_ref[...] = pout[...]

    @pl.when(strip != me)
    def _():
        to_mid.wait_send()
        hand_over.wait()
        pred_ref[...] = pin[...]

    @pl.when(me < tiles - 1)
    def _():
        to_up.wait_send()

    @pl.when(me > 0)
    def _():
        to_down.wait_send()

    @pl.when(has_up)
    def _():
        for copy in grid_up:
            copy.wait_send()

    @pl.when(has_down)
    def _():
        for copy in grid_down:
            copy.wait_send()

    def sent(k, carry):
        peer = tile_peer(k)
        wave_copy(peer, me).wait_send()
        bin_copy(peer, me).wait_send()
        return carry

    lax.fori_loop(1, tiles, sent, 0)
    for a in range(chunks + 1):
        swap(a).wait_send()

    def handed(k):
        share_copy(lax.rem(chip + k, groups), chip).wait_send()

    repeat(groups - 1, lambda n: handed(n + 1))

    square[...] = jnp.zeros(square.shape, F32)
    count = 9 * piece

    def keep(h, p):
        even = decode(gathered[h, 2 * p], 0)
        odd = decode(gathered[h, 2 * p + 1], 1)
        tiles = [even[8 * t : 8 * t + 8] for t in range(whole // 8)]
        tiles.append(jnp.where(top, even[whole:], odd[whole:]))
        tiles += [odd[8 * t : 8 * t + 8] for t in range(whole // 8)]
        total_sq = square[h]
        for t, tile in enumerate(tiles):
            at = h * count + p * per_pair + 8 * t
            raw_ref[at // steps, pl.ds(pl.multiple_of(at % steps, 8), 8), :] = tile
            total_sq = total_sq + tile * tile
        square[h] = total_sq

    def keep_pair(h, p):
        if isinstance(p, int):
            if p * per_pair < count:
                keep(h, p)
        else:
            pl.when(p * per_pair < count)(lambda: keep(h, p))

    def take(p):
        for q in (2 * p, 2 * p + 1):

            @pl.when(chip != q)
            def _():
                spread_copy(device_at(q), q).wait_recv()
                forward(q, core).start()

        keep_pair(core, p)

    repeat(groups // 2, take)

    def shared(k, carry):
        q, device = group_peer(k)
        spread_copy(device, q).wait_send()
        return carry

    repeat(groups - 1, lambda n: shared(n + 1, 0))

    def fetch(p):
        for q in (2 * p, 2 * p + 1):
            forward(q, 1 - core).wait_recv()
        keep_pair(1 - core, p)

    repeat(groups // 2, fetch)
    extra_ref[10:16, :] = jnp.zeros((6, channels), F32) + 1.0 / jnp.sqrt(
        jnp.sum(square[0] + square[1]) / (9 * steps * channels) + 1e-06
    )
    smalls = []
    for p in range(3):
        smalls.append(jnp.where(top, decode(gathered[0, 2 * p + 1], 1)[whole:], decode(gathered[0, 2 * p], 0)[whole:]))
    rows = []
    for n in range(10):
        at = small_row(n)
        rows.append(smalls[at // 8][at % 8 : at % 8 + 1])
    two = jnp.zeros((1, channels), F32)
    for row in rows[:9]:
        two = two + row * row
    scale_two = 1.0 / jnp.sqrt(jnp.sum(two) / (9 * channels) + 1e-06)
    for n in range(9):
        extra_ref[n : n + 1, :] = rows[n] * scale_two
    extra_ref[9:10, :] = rows[9] / jnp.sqrt(jnp.sum(rows[9] * rows[9]) / channels + 1e-06)

    def passed(q, carry):
        forward(q, core).wait_send()
        return carry

    repeat(groups, lambda q: passed(q, 0))


def finish_kernel(pred_ref, raw_ref, extra_ref, pred_out, u1_out, ub_out, u2_out, u1, ub, u2, sem):
    copies = [
        pltpu.make_async_copy(src, dst, sem.at[k])
        for k, (src, dst) in enumerate([(pred_ref, pred_out), (ub, ub_out), (u2, u2_out)])
    ]
    copies[0].start()
    scale = extra_ref[10:11, :]
    for i in range(3):
        for k in range(3 * i, 3 * i + 3):
            u1[k] = raw_ref[k] * scale
        copies.append(pltpu.make_async_copy(u1.at[pl.ds(3 * i, 3)], u1_out.at[i], sem.at[3 + i]))
        copies[-1].start()
    ub[...] = extra_ref[9:10, :]
    for n in range(9):
        u2[n // 3, n % 3 : n % 3 + 1, :] = extra_ref[n : n + 1, :]
    copies[1].start()
    copies[2].start()
    for copy in copies:
        copy.wait()


def on_device(tiles, reps, waves, dest_tile, pixel_bin, target, conv_one, bias_one, conv_two, bias_two):
    rows, steps = waves.shape[1:]
    height, width = target.shape[1:]
    channels = conv_one.shape[3]
    pixels = height * width
    groups = tiles // 2 * reps
    units = -(-9 * (steps // 8) // groups) // 2 * 2 + 1
    part = 4 * units + 4
    padded = (pair_rows(part) + 8) * (groups // 2)
    hbm = pl.BlockSpec(memory_space=pltpu.HBM)
    tp = -(-(height + 2) // 8) * 8
    dma = pltpu.SemaphoreType.DMA
    vmem = pl.BlockSpec(memory_space=pltpu.VMEM)
    held = pl.pallas_call(
        functools.partial(step_kernel, tiles, reps, part),
        out_shape=(
            pltpu.VMEM((height, width), F32),
            pltpu.VMEM((9, steps, channels), F32),
            pltpu.VMEM((16, channels), F32),
        ),
        in_specs=[hbm] * 8,
        out_specs=(vmem,) * 3,
        scratch_shapes=[
            pltpu.VMEM((1, rows), jnp.int32),
            pltpu.VMEM((1, rows), jnp.int32),
            pltpu.VMEM((rows, steps), BF16),
            pltpu.VMEM((height, width), F32),
            pltpu.VMEM((3, 3 * steps, channels), BF16),
            pltpu.VMEM((1, channels), F32),
            pltpu.VMEM((3, 3, channels), BF16),
            pltpu.VMEM((1, 1), F32),
            dma((8,)),
            pltpu.VMEM((tiles * CAP, steps), BF16),
            pltpu.VMEM((tiles, 1, 128), F32),
            pltpu.VMEM((tiles * CAP, steps), BF16),
            pltpu.VMEM((tiles, 1, 128), F32),
            pltpu.VMEM(((height + 2 * HALO) * width, steps), BF16),
            pltpu.VMEM(((height + 2 * HALO) * width, 3 * steps), BF16),
            pltpu.VMEM((pixels, channels), F32),
            pltpu.VMEM(((height + HALO) * width, channels), BF16),
            pltpu.VMEM(((height + HALO) * width, channels), F32),
            pltpu.VMEM((height, width), F32),
            pltpu.VMEM((height, width), F32),
            pltpu.VMEM((height, width), F32),
            pltpu.VMEM((height, width), F32),
            pltpu.VMEM((height, width), F32),
            pltpu.VMEM((24, channels), F32),
            pltpu.VMEM((5, tp, width), F32),
            pltpu.VMEM((24, pixels), F32),
            pltpu.VMEM((2, padded, channels), F32),
            pltpu.VMEM((padded, channels), F32),
            pltpu.VMEM((part, channels), F32),
            pltpu.VMEM((groups, part, channels), jnp.int16),
            pltpu.VMEM((groups, part, channels), jnp.int16),
            pltpu.VMEM((2, groups, part, channels), jnp.int16),
            pltpu.VMEM((2, 8, channels), F32),
            dma((tiles,)), dma((tiles,)), dma((tiles,)), dma((tiles,)),
            dma((4,)), dma((4,)), dma((4,)), dma((4,)),
            dma((CHUNKS + 1,)), dma((CHUNKS + 1,)), dma((groups,)), dma((groups,)),
            dma((groups,)), dma((groups,)), dma((groups,)), dma((groups,)),
        ],
        compiler_params=pltpu.CompilerParams(
            collective_id=0, has_side_effects=True, vmem_limit_bytes=58 * 1024 * 1024
        ),
        name="step",
    )(
        dest_tile.reshape(1, rows), pixel_bin, waves[0], target[0],
        conv_one.reshape(3, 3 * steps, channels), bias_one.reshape(1, channels), conv_two, bias_two.reshape(1, 1),
    )
    pred, one, bias, two = pl.pallas_call(
        finish_kernel,
        out_shape=(
            jax.ShapeDtypeStruct((height, width), F32),
            jax.ShapeDtypeStruct((3, 3, steps, channels), F32),
            jax.ShapeDtypeStruct((1, channels), F32),
            jax.ShapeDtypeStruct((3, 3, channels), F32),
        ),
        in_specs=[vmem] * 3,
        out_specs=(hbm,) * 4,
        scratch_shapes=[
            pltpu.VMEM((9, steps, channels), F32),
            pltpu.VMEM((1, channels), F32),
            pltpu.VMEM((3, 3, channels), F32),
            dma((12,)),
        ],
        name="finish",
    )(*[pltpu.with_memory_space_constraint(x, pltpu.VMEM) for x in held])
    return pred[None], one, bias[0], two


def solution(mesh):
    placed = (
        P("rep", "tile", None),
        P("rep", "tile", None),
        P("rep", "tile"),
        P("rep", "tile", None),
        P(),
        P(),
        P(),
        P(),
    )
    return jax.shard_map(
        functools.partial(on_device, mesh.shape["tile"], mesh.shape["rep"]),
        mesh=mesh,
        in_specs=placed,
        out_specs=(P("rep", "tile", None), P(), P(), P()),
        check_vma=False,
    )
```

```python
import functools

import jax
import jax.numpy as jnp
from jax import lax
from jax.experimental import pallas as pl
from jax.experimental.pallas import tpu as pltpu
from jax.sharding import PartitionSpec as P

CAP = 32
HALO = 4
CHUNKS = 4
LEVELS = 32000.0
MESH = pl.DeviceIdType.MESH
F32 = jnp.float32
BF16 = jnp.bfloat16


def iota(shape, dim):
    return lax.broadcasted_iota(jnp.int32, shape, dim)


def dot(a, b, dims=((1,), (0,))):
    return lax.dot_general(a, b, (dims, ((), ())), preferred_element_type=F32)


def repeat(count, body):
    if count <= 16:
        for n in range(count):
            body(n)
    else:

        def step(n, carry):
            body(n)
            return carry

        lax.fori_loop(0, count, step, 0)


def pair_rows(part):
    return 2 * part - 8


def small_row(n):
    return 8 * (n // 4) + (2 if n // 2 % 2 else 6) + n % 2


def exponent(largest):
    largest = jnp.maximum(jnp.max(largest, axis=0, keepdims=True), 2.0**-100)
    return jnp.ceil(jnp.log2(largest))


def encode(value, odd):
    last = value[-8:]
    row = iota(last.shape, 0)
    own = (row >= 4) == (odd == 1)
    inner = row - jnp.where(row >= 4, 4, 0)
    size = jnp.abs(last)
    largest = jnp.where(own, size, 0.0)
    for t in range(value.shape[0] // 8 - 1):
        largest = jnp.maximum(largest, jnp.abs(value[8 * t : 8 * t + 8]))
    one = exponent(largest)
    two = exponent(jnp.where(jnp.logical_or(own, inner < 2), 0.0, size))
    by_one = jnp.exp2(-one) * LEVELS
    by_two = jnp.exp2(-two) * LEVELS
    last = jnp.where(
        own, last * by_one, jnp.where(inner == 0, one, jnp.where(inner == 1, two, last * by_two))
    )
    if value.shape[0] > 8:
        last = jnp.concatenate([value[:-8] * by_one, last], axis=0)
    return jnp.round(last).astype(jnp.int32).astype(jnp.int16)


def decode(code, odd):
    value = code.astype(jnp.int32).astype(F32)
    last = value[-8:]
    own = (iota(last.shape, 0) >= 4) == (odd == 1)
    if isinstance(odd, int):
        one, two = (last[0:1], last[1:2]) if odd else (last[4:5], last[5:6])
    else:
        one = jnp.where(odd == 1, last[0:1], last[4:5])
        two = jnp.where(odd == 1, last[1:2], last[5:6])
    by_one = jnp.exp2(one) * (1.0 / LEVELS)
    last = last * jnp.where(own, by_one, jnp.exp2(two) * (1.0 / LEVELS))
    return jnp.concatenate([value[:-8] * by_one, last], axis=0) if value.shape[0] > 8 else last


def sum_shares(codes, odd):
    count = codes.shape[0]
    if count <= 16:
        out = decode(codes[0], odd)
        for s in range(1, count):
            out = out + decode(codes[s], odd)
        return out
    return lax.fori_loop(
        0, count, lambda s, out: out + decode(codes[s], odd), jnp.zeros(codes.shape[1:], F32)
    )


def holder(strip):
    pair, chip = strip // 4, strip // 2
    turned = 2 * pair + lax.rem(chip + pair, 2)
    return 2 * turned + lax.rem(strip, 2)


def step_kernel(
    tiles, reps, part,
    dest_hbm, bin_hbm, waves_hbm, target_hbm, w1_hbm, b1_hbm, w2_hbm, b2_hbm,
    pred_ref, raw_ref, extra_ref,
    dest_ref, bin_ref, waves_ref, target_ref, w1_ref, b1_ref, w2_ref, b2_ref, l_sem,
    sendw, sendb, recvw, recvb, grid, wide, pre_s, hid_s, acc_s, tlow, thigh, tmid, pout, pin, w2_s, taps, etap,
    full, pair, total, coded, recva, gathered, square,
    aw_send, aw_recv, ab_send, ab_recv, t_send, t_recv, g_send, g_recv,
    p_send, p_recv, s_send, s_recv, n_send, n_recv, f_send, f_recv,
):
    me = lax.axis_index("tile")
    rep = lax.axis_index("rep")
    rows, steps = waves_ref.shape
    height, width = target_ref.shape
    channels = b1_ref.shape[1]
    half = tiles // 2
    groups = half * reps
    core = lax.rem(me, 2)
    partner = me + 1 - 2 * core
    stride = half // 2 + 1
    chip = lax.rem(me // 2 * stride, half) * reps + rep
    strip = holder(me)
    chunks = CHUNKS
    pixels = height * width
    tall = height + HALO

    def tile_peer(k):
        return lax.rem(me + k, tiles)

    def group_peer(k):
        q = lax.rem(chip + k, groups)
        return q, device_at(q)

    def device_at(q):
        return {"tile": 2 * lax.rem(q // reps * stride, half) + core, "rep": lax.rem(q, reps)}

    loads = [
        pltpu.make_async_copy(src, dst, l_sem.at[k])
        for k, (src, dst) in enumerate(
            [
                (dest_hbm, dest_ref), (bin_hbm, bin_ref), (waves_hbm, waves_ref), (target_hbm, target_ref),
                (w1_hbm, w1_ref), (b1_hbm, b1_ref), (w2_hbm, w2_ref), (b2_hbm, b2_ref),
            ]
        )
    ]
    for load in loads:
        load.start()

    barrier = pltpu.get_barrier_semaphore()

    def greet(k, carry):
        pl.semaphore_signal(barrier, inc=1, device_id={"tile": tile_peer(k), "rep": rep}, device_id_type=MESH)
        return carry

    repeat(tiles - 1, lambda n: greet(n + 1, 0))

    def greet_far(k, carry):
        pl.semaphore_signal(
            barrier,
            inc=1,
            device_id={"tile": 2 * lax.rem(k, half) + core, "rep": lax.rem(rep + 1 + k // half, reps)},
            device_id_type=MESH,
        )
        return carry

    repeat((reps - 1) * half, lambda n: greet_far(n, 0))

    for load in loads[:4]:
        load.wait()

    hits = (iota((tiles, rows), 0) == dest_ref[...]).astype(F32)
    earlier = (iota((rows, rows), 0) < iota((rows, rows), 1)).astype(F32).astype(BF16)
    ranks = dot(hits.astype(BF16), earlier)
    rank = jnp.sum(hits * ranks, axis=0, keepdims=True)
    slot = jnp.sum(hits * (ranks + (CAP * iota((tiles, rows), 0)).astype(F32)), axis=0, keepdims=True)
    place = (iota((tiles * CAP, rows), 0).astype(F32) == slot).astype(F32).astype(BF16)
    sendw[...] = dot(place, waves_ref[...]).astype(BF16)
    lane = rank + (CAP * lax.rem(me, 4)).astype(F32)
    lanes = (iota((128, rows), 0).astype(F32) == lane).astype(F32).astype(BF16)
    bins = bin_ref[...]
    high = (bins // 32).astype(F32)
    low = (bins - 32 * (bins // 32)).astype(F32)
    named = 32.0 * dot((hits * high).astype(BF16), lanes, ((1,), (1,))) + dot(
        (hits * low).astype(BF16), lanes, ((1,), (1,))
    )
    for t in range(tiles):
        sendb[t] = named[t : t + 1, :]

    pl.semaphore_wait(barrier, tiles - 1 + (reps - 1) * half)

    def wave_copy(peer, source):
        return pltpu.make_async_remote_copy(
            src_ref=sendw.at[pl.ds(pl.multiple_of(holder(peer) * CAP, CAP), CAP)],
            dst_ref=recvw.at[pl.ds(pl.multiple_of(source * CAP, CAP), CAP)],
            send_sem=aw_send.at[peer],
            recv_sem=aw_recv.at[source],
            device_id={"tile": peer, "rep": rep},
            device_id_type=MESH,
        )

    def bin_copy(peer, source):
        return pltpu.make_async_remote_copy(
            src_ref=sendb.at[holder(peer)],
            dst_ref=recvb.at[source],
            send_sem=ab_send.at[peer],
            recv_sem=ab_recv.at[source],
            device_id={"tile": peer, "rep": rep},
            device_id_type=MESH,
        )

    def scatter(k, carry):
        peer = tile_peer(k)
        wave_copy(peer, me).start()
        bin_copy(peer, me).start()
        return carry

    lax.fori_loop(1, tiles, scatter, 0)

    def target_copy(peer, dst, k):
        return pltpu.make_async_remote_copy(
            src_ref=target_ref, dst_ref=dst, send_sem=t_send.at[k], recv_sem=t_recv.at[k],
            device_id={"tile": peer, "rep": rep}, device_id_type=MESH,
        )

    has_up = strip < tiles - 1
    has_down = strip > 0
    up = holder(jnp.minimum(strip + 1, tiles - 1))
    down = holder(jnp.maximum(strip - 1, 0))
    span = HALO * width
    step_px = 2 * width

    def halo_copy(peer, src, dst, k):
        return pltpu.make_async_remote_copy(
            src_ref=grid.at[pl.ds(src * width, step_px)], dst_ref=grid.at[pl.ds(dst * width, step_px)],
            send_sem=g_send.at[k], recv_sem=g_recv.at[k],
            device_id={"tile": peer, "rep": rep}, device_id_type=MESH,
        )

    to_up = target_copy(holder(jnp.minimum(me + 1, tiles - 1)), tlow, 0)
    to_down = target_copy(holder(jnp.maximum(me - 1, 0)), thigh, 1)
    to_mid = target_copy(strip, tmid, 2)
    grid_up = [halo_copy(up, height + 2, 2, 0), halo_copy(up, height, 0, 1)]
    grid_down = [halo_copy(down, HALO, height + HALO, 2), halo_copy(down, HALO + 2, height + HALO + 2, 3)]

    @pl.when(me < tiles - 1)
    def _():
        to_up.start()

    @pl.when(me > 0)
    def _():
        to_down.start()

    @pl.when(strip != me)
    def _():
        to_mid.start()

    @pl.when(strip == me)
    def _():
        tmid[...] = target_ref[...]

    @pl.when(jnp.logical_not(has_down))
    def _():
        grid[0:span, :] = jnp.zeros((span, steps), BF16)
        tlow[...] = jnp.zeros((height, width), F32)

    @pl.when(jnp.logical_not(has_up))
    def _():
        grid[span + pixels : span + pixels + span, :] = jnp.zeros((span, steps), BF16)
        thigh[...] = jnp.zeros((height, width), F32)

    own = pl.ds(pl.multiple_of(me * CAP, CAP), CAP)
    recvw[own, :] = sendw[pl.ds(pl.multiple_of(strip * CAP, CAP), CAP), :]
    recvb[me] = sendb[strip]
    for load in loads[4:]:
        load.wait()
    w2_s[...] = jnp.zeros(w2_s.shape, F32)
    for i in range(3):
        w2_s[8 * i : 8 * i + 3, :] = w2_ref[i].astype(F32)
    w2 = w2_s[...].astype(BF16)

    def arrive(k, carry):
        peer = tile_peer(k)
        wave_copy(peer, peer).wait_recv()
        bin_copy(peer, peer).wait_recv()
        return carry

    lax.fori_loop(1, tiles, arrive, 0)

    names = []
    for q in range(tiles // 4):
        names.append(recvb[4 * q] + recvb[4 * q + 1] + recvb[4 * q + 2] + recvb[4 * q + 3])
    names = jnp.concatenate(names, axis=1)
    stages = [(height - 2, has_up, grid_up[0]), (0, has_down, grid_down[0])]
    stages += [(height - 4, has_up, grid_up[1]), (2, has_down, grid_down[1])]
    stages += [(y, None, None) for y in range(HALO, height - HALO, 2)]
    for y, there, copy in stages:
        wanted = (iota((step_px, tiles * CAP), 0) + y * width).astype(F32)
        onehot = (wanted == names).astype(F32).astype(BF16)
        grid[span + y * width : span + y * width + step_px, :] = dot(onehot, recvw[...]).astype(BF16)
        if copy is not None:
            pl.when(there)(copy.start)

    column = iota((width, steps), 0)

    def spread(y):
        line = grid[y * width : (y + 1) * width, :]
        value = line.astype(F32)
        left = jnp.where(column >= 2, pltpu.roll(value, 2, 0), 0.0)
        right = jnp.where(column < width - 2, pltpu.roll(value, width - 2, 0), 0.0)
        wide[y * width : (y + 1) * width, 0:steps] = left.astype(BF16)
        wide[y * width : (y + 1) * width, steps : 2 * steps] = line
        wide[y * width : (y + 1) * width, 2 * steps : 3 * steps] = right.astype(BF16)

    for y in range(HALO, HALO + height):
        spread(y)

    bias = b1_ref[...]

    def convolve(y, terms, first, last):
        acc = jnp.zeros((step_px, channels), F32) + bias if first else acc_s[y * width : (y + 2) * width, :]
        for i in terms:
            acc = acc + dot(wide[(y + 2 * i) * width : (y + 2 * i + 2) * width, :], w1_ref[i])
        if not last:
            acc_s[y * width : (y + 2) * width, :] = acc
            return
        sig = 1.0 / (1.0 + jnp.exp(-acc))
        hidden = acc * sig
        if y < 2:
            hidden = jnp.where(has_down, hidden, 0.0)
        if y >= height + 2:
            hidden = jnp.where(has_up, hidden, 0.0)
        hid_s[y * width : (y + 2) * width, :] = hidden.astype(BF16)
        if 2 <= y < height + 2:
            pre_s[(y - 2) * width : y * width, :] = sig * (1.0 + acc * (1.0 - sig))

    begun = set()

    def advance(rows):
        for y in range(0, tall, 2):
            terms = [i for i in range(3) if y + 2 * i in rows]
            if terms:
                done[y] = done.get(y, 0) + len(terms)
                convolve(y, terms, y not in begun, done[y] == 3)
                begun.add(y)

    done = {}
    advance(range(HALO, HALO + height, 2))
    for k in range(2):

        @pl.when(has_down)
        def _():
            grid_up[k].wait_recv()

        @pl.when(has_up)
        def _():
            grid_down[k].wait_recv()

        fresh = [2 - 2 * k, height + HALO + 2 * k]
        for y in fresh:
            spread(y)
            spread(y + 1)
        advance(fresh)

    each = dot(w2, hid_s[...], ((1,), (1,)))
    span2 = (height + 2) * width
    summed = each[0:8, 0:span2] + each[8:16, width : width + span2] + each[16:24, 2 * width : 2 * width + span2]
    taps[...] = jnp.zeros(taps.shape, F32)
    for y in range(height + 2):
        for j in range(3):
            taps[j, y : y + 1, :] = summed[j : j + 1, y * width : (y + 1) * width]
    tp = taps.shape[1]
    x_at = iota((tp, width), 1)
    y_at = iota((tp, width), 0)
    pred = (
        b2_ref[...]
        + jnp.where(x_at >= 1, pltpu.roll(taps[0], 1, 1), 0.0)
        + taps[1]
        + jnp.where(x_at < width - 1, pltpu.roll(taps[2], width - 1, 1), 0.0)
    )

    @pl.when(has_down)
    def _():
        to_up.wait_recv()

    @pl.when(has_up)
    def _():
        to_down.wait_recv()

    @pl.when(strip != me)
    def _():
        to_mid.wait_recv()

    taps[3] = pred
    pout[...] = taps[3, 1 : 1 + height, :]
    hand_over = pltpu.make_async_remote_copy(
        src_ref=pout, dst_ref=pin, send_sem=t_send.at[3], recv_sem=t_recv.at[3],
        device_id={"tile": strip, "rep": rep}, device_id_type=MESH,
    )
    pl.when(strip != me)(hand_over.start)
    taps[4, 0:1, :] = tlow[height - 1 : height, :]
    taps[4, 1 : 1 + height, :] = tmid[...]
    taps[4, 1 + height : 2 + height, :] = thigh[0:1, :]
    inside = jnp.logical_and(
        jnp.logical_or(y_at >= 1, has_down),
        jnp.logical_and(y_at < height + 2, jnp.logical_or(y_at < height + 1, has_up)),
    )
    error = jnp.where(inside, (pred - taps[4]) / reps, 0.0).astype(BF16).astype(F32)
    taps[0] = jnp.where(x_at < width - 1, pltpu.roll(error, width - 1, 1), 0.0)
    taps[1] = error
    taps[2] = jnp.where(x_at >= 1, pltpu.roll(error, 1, 1), 0.0)
    etap[...] = jnp.zeros(etap.shape, F32)
    for i in range(3):
        for j in range(3):
            for y in range(height):
                etap[8 * i + j : 8 * i + j + 1, y * width : (y + 1) * width] = taps[j, y + 2 - i : y + 3 - i, :]
    errors = etap[...].astype(BF16)

    mine = hid_s[2 * width : 2 * width + pixels, :]
    grad_two = dot(errors, mine)
    back = dot(errors, w2, ((0,), (0,)))
    slope = (back * pre_s[...]).astype(BF16)
    grad_bias = dot(jnp.ones((8, pixels), BF16), slope)
    piece = steps // 2
    data = 9 * piece
    spare = pair_rows(part) * (groups // 2)
    for h in range(2):
        if spare > data:
            full[h, data:spare, :] = jnp.zeros((spare - data, channels), F32)
        full[h, spare:, :] = jnp.zeros((full.shape[1] - spare, channels), F32)
        for n in range(10):
            at = spare + small_row(n)
            full[h, at : at + 1, :] = grad_two[8 * (n // 3) + n % 3 :, :][0:1] if n < 9 else grad_bias[0:1]
    slab = spare // chunks

    def swap(a):
        rows_a = pl.ds(a * slab, slab) if a < chunks else pl.ds(spare, full.shape[1] - spare)
        return pltpu.make_async_remote_copy(
            src_ref=full.at[1 - core, rows_a], dst_ref=pair.at[rows_a],
            send_sem=p_send.at[a], recv_sem=p_recv.at[a],
            device_id={"tile": partner, "rep": rep}, device_id_type=MESH,
        )

    swap(chunks).start()
    started = 0
    for i in range(3):
        start = (2 + 2 * i) * width
        g = dot(wide[start : start + pixels, :], slope, ((0,), (0,)))
        for j in range(3):
            k = 3 * i + j
            for h in range(2):
                full[h, k * piece : (k + 1) * piece, :] = g[j * steps + h * piece : j * steps + (h + 1) * piece, :]
        while started < chunks and ((started + 1) * slab <= 3 * (i + 1) * piece or i == 2):
            swap(started).start()
            started += 1

    def share_copy(q, source):
        return pltpu.make_async_remote_copy(
            src_ref=coded.at[q], dst_ref=recva.at[source],
            send_sem=s_send.at[q], recv_sem=s_recv.at[source],
            device_id=device_at(q), device_id_type=MESH,
        )

    whole = part - 8
    per_pair = pair_rows(part)
    top = iota((8, channels), 0) < 4

    def hand_out(p):
        rows_p = pl.ds(p * per_pair, per_pair)
        rows_s = pl.ds(spare + p * 8, 8)
        x = full[core, rows_p, :] + pair[rows_p, :]
        extra = full[core, rows_s, :] + pair[rows_s, :]
        for odd in range(2):
            q = 2 * p + odd
            mixed = x[whole : whole + 8]
            mixed = jnp.where(top, extra, mixed) if odd else jnp.where(top, mixed, extra)
            value = x[whole + 8 :] if odd else x[:whole]
            value = jnp.concatenate([value, mixed], axis=0) if whole else mixed

            @pl.when(chip == q)
            def _():
                total[...] = value

            @pl.when(chip != q)
            def _():
                coded[q] = encode(value, odd)
                share_copy(q, chip).start()

    swap(chunks).wait_recv()
    pairs_each = groups // 2 // chunks
    for a in range(chunks):
        swap(a).wait_recv()
        repeat(pairs_each, lambda n: hand_out(a * pairs_each + n))

    def arrived(k):
        share_copy(lax.rem(chip + k, groups), lax.rem(chip + groups - k, groups)).wait_recv()

    repeat(groups - 1, lambda n: arrived(n + 1))
    parity = lax.rem(chip, 2)
    recva[chip] = jnp.zeros(recva.shape[1:], recva.dtype)
    total[...] = total[...] + sum_shares(recva, parity)
    gathered[core, chip] = encode(total[...], parity)

    def spread_copy(device, source):
        return pltpu.make_async_remote_copy(
            src_ref=gathered.at[core, chip], dst_ref=gathered.at[core, source],
            send_sem=n_send.at[source], recv_sem=n_recv.at[source], device_id=device, device_id_type=MESH,
        )

    def spread_to(q):
        @pl.when(chip != q)
        def _():
            pltpu.make_async_remote_copy(
                src_ref=gathered.at[core, chip], dst_ref=gathered.at[core, chip],
                send_sem=n_send.at[q], recv_sem=n_recv.at[chip], device_id=device_at(q), device_id_type=MESH,
            ).start()

    repeat(groups, spread_to)

    def forward(q, which):
        return pltpu.make_async_remote_copy(
            src_ref=gathered.at[which, q], dst_ref=gathered.at[which, q],
            send_sem=f_send.at[q], recv_sem=f_recv.at[q],
            device_id={"tile": partner, "rep": rep}, device_id_type=MESH,
        )

    forward(chip, core).start()

    @pl.when(strip == me)
    def _():
        pred_ref[...] = pout[...]

    @pl.when(strip != me)
    def _():
        to_mid.wait_send()
        hand_over.wait()
        pred_ref[...] = pin[...]

    @pl.when(me < tiles - 1)
    def _():
        to_up.wait_send()

    @pl.when(me > 0)
    def _():
        to_down.wait_send()

    @pl.when(has_up)
    def _():
        for copy in grid_up:
            copy.wait_send()

    @pl.when(has_down)
    def _():
        for copy in grid_down:
            copy.wait_send()

    def sent(k, carry):
        peer = tile_peer(k)
        wave_copy(peer, me).wait_send()
        bin_copy(peer, me).wait_send()
        return carry

    lax.fori_loop(1, tiles, sent, 0)
    for a in range(chunks + 1):
        swap(a).wait_send()

    def handed(k):
        share_copy(lax.rem(chip + k, groups), chip).wait_send()

    repeat(groups - 1, lambda n: handed(n + 1))

    square[...] = jnp.zeros(square.shape, F32)
    count = 9 * piece

    def keep(h, p):
        even = decode(gathered[h, 2 * p], 0)
        odd = decode(gathered[h, 2 * p + 1], 1)
        tiles = [even[8 * t : 8 * t + 8] for t in range(whole // 8)]
        tiles.append(jnp.where(top, even[whole:], odd[whole:]))
        tiles += [odd[8 * t : 8 * t + 8] for t in range(whole // 8)]
        total_sq = square[h]
        for t, tile in enumerate(tiles):
            at = p * per_pair + 8 * t
            k, r = at // piece, at % piece
            raw_ref[k, pl.ds(pl.multiple_of(h * piece + r, 8), 8), :] = tile
            total_sq = total_sq + tile * tile
        square[h] = total_sq

    def keep_pair(h, p):
        if isinstance(p, int):
            if p * per_pair < count:
                keep(h, p)
        else:
            pl.when(p * per_pair < count)(lambda: keep(h, p))

    def take(p):
        for q in (2 * p, 2 * p + 1):

            @pl.when(chip != q)
            def _():
                spread_copy(device_at(q), q).wait_recv()
                forward(q, core).start()

        keep_pair(core, p)

    repeat(groups // 2, take)

    def shared(k, carry):
        q, device = group_peer(k)
        spread_copy(device, q).wait_send()
        return carry

    repeat(groups - 1, lambda n: shared(n + 1, 0))

    def small_updates():
        smalls = []
        for p in range(3):
            smalls.append(jnp.where(top, decode(gathered[0, 2 * p + 1], 1)[whole:], decode(gathered[0, 2 * p], 0)[whole:]))
        rows = []
        for n in range(10):
            at = small_row(n)
            rows.append(smalls[at // 8][at % 8 : at % 8 + 1])
        two = jnp.zeros((1, channels), F32)
        for row in rows[:9]:
            two = two + row * row
        scale_two = 1.0 / jnp.sqrt(jnp.sum(two) / (9 * channels) + 1e-06)
        for n in range(9):
            extra_ref[n : n + 1, :] = rows[n] * scale_two
        extra_ref[9:10, :] = rows[9] / jnp.sqrt(jnp.sum(rows[9] * rows[9]) / channels + 1e-06)

    def fetch(p):
        for q in (2 * p, 2 * p + 1):
            forward(q, 1 - core).wait_recv()
        keep_pair(1 - core, p)

    for p in range(3):
        fetch(p)
    small_updates()
    repeat(groups // 2 - 3, lambda n: fetch(n + 3))
    extra_ref[10:16, :] = jnp.zeros((6, channels), F32) + 1.0 / jnp.sqrt(
        jnp.sum(square[0] + square[1]) / (9 * steps * channels) + 1e-06
    )
    def passed(q, carry):
        forward(q, core).wait_send()
        return carry

    repeat(groups, lambda q: passed(q, 0))


def finish_kernel(pred_ref, raw_ref, extra_ref, pred_out, u1_out, ub_out, u2_out, u1, ub, u2, sem):
    copies = [
        pltpu.make_async_copy(src, dst, sem.at[k])
        for k, (src, dst) in enumerate([(pred_ref, pred_out), (ub, ub_out), (u2, u2_out)])
    ]
    copies[0].start()
    scale = extra_ref[10:11, :]
    for i in range(3):
        for k in range(3 * i, 3 * i + 3):
            u1[k] = raw_ref[k] * scale
        copies.append(pltpu.make_async_copy(u1.at[pl.ds(3 * i, 3)], u1_out.at[i], sem.at[3 + i]))
        copies[-1].start()
    ub[...] = extra_ref[9:10, :]
    for n in range(9):
        u2[n // 3, n % 3 : n % 3 + 1, :] = extra_ref[n : n + 1, :]
    copies[1].start()
    copies[2].start()
    for copy in copies:
        copy.wait()


def on_device(tiles, reps, waves, dest_tile, pixel_bin, target, conv_one, bias_one, conv_two, bias_two):
    rows, steps = waves.shape[1:]
    height, width = target.shape[1:]
    channels = conv_one.shape[3]
    pixels = height * width
    groups = tiles // 2 * reps
    units = -(-9 * (steps // 8) // groups) // 2 * 2 + 1
    part = 4 * units + 4
    padded = (pair_rows(part) + 8) * (groups // 2)
    hbm = pl.BlockSpec(memory_space=pltpu.HBM)
    tp = -(-(height + 2) // 8) * 8
    dma = pltpu.SemaphoreType.DMA
    vmem = pl.BlockSpec(memory_space=pltpu.VMEM)
    held = pl.pallas_call(
        functools.partial(step_kernel, tiles, reps, part),
        out_shape=(
            pltpu.VMEM((height, width), F32),
            pltpu.VMEM((9, steps, channels), F32),
            pltpu.VMEM((16, channels), F32),
        ),
        in_specs=[hbm] * 8,
        out_specs=(vmem,) * 3,
        scratch_shapes=[
            pltpu.VMEM((1, rows), jnp.int32),
            pltpu.VMEM((1, rows), jnp.int32),
            pltpu.VMEM((rows, steps), BF16),
            pltpu.VMEM((height, width), F32),
            pltpu.VMEM((3, 3 * steps, channels), BF16),
            pltpu.VMEM((1, channels), F32),
            pltpu.VMEM((3, 3, channels), BF16),
            pltpu.VMEM((1, 1), F32),
            dma((8,)),
            pltpu.VMEM((tiles * CAP, steps), BF16),
            pltpu.VMEM((tiles, 1, 128), F32),
            pltpu.VMEM((tiles * CAP, steps), BF16),
            pltpu.VMEM((tiles, 1, 128), F32),
            pltpu.VMEM(((height + 2 * HALO) * width, steps), BF16),
            pltpu.VMEM(((height + 2 * HALO) * width, 3 * steps), BF16),
            pltpu.VMEM((pixels, channels), F32),
            pltpu.VMEM(((height + HALO) * width, channels), BF16),
            pltpu.VMEM(((height + HALO) * width, channels), F32),
            pltpu.VMEM((height, width), F32),
            pltpu.VMEM((height, width), F32),
            pltpu.VMEM((height, width), F32),
            pltpu.VMEM((height, width), F32),
            pltpu.VMEM((height, width), F32),
            pltpu.VMEM((24, channels), F32),
            pltpu.VMEM((5, tp, width), F32),
            pltpu.VMEM((24, pixels), F32),
            pltpu.VMEM((2, padded, channels), F32),
            pltpu.VMEM((padded, channels), F32),
            pltpu.VMEM((part, channels), F32),
            pltpu.VMEM((groups, part, channels), jnp.int16),
            pltpu.VMEM((groups, part, channels), jnp.int16),
            pltpu.VMEM((2, groups, part, channels), jnp.int16),
            pltpu.VMEM((2, 8, channels), F32),
            dma((tiles,)), dma((tiles,)), dma((tiles,)), dma((tiles,)),
            dma((4,)), dma((4,)), dma((4,)), dma((4,)),
            dma((CHUNKS + 1,)), dma((CHUNKS + 1,)), dma((groups,)), dma((groups,)),
            dma((groups,)), dma((groups,)), dma((groups,)), dma((groups,)),
        ],
        compiler_params=pltpu.CompilerParams(
            collective_id=0, has_side_effects=True, vmem_limit_bytes=58 * 1024 * 1024
        ),
        name="step",
    )(
        dest_tile.reshape(1, rows), pixel_bin, waves[0], target[0],
        conv_one.reshape(3, 3 * steps, channels), bias_one.reshape(1, channels), conv_two, bias_two.reshape(1, 1),
    )
    pred, one, bias, two = pl.pallas_call(
        finish_kernel,
        out_shape=(
            jax.ShapeDtypeStruct((height, width), F32),
            jax.ShapeDtypeStruct((3, 3, steps, channels), F32),
            jax.ShapeDtypeStruct((1, channels), F32),
            jax.ShapeDtypeStruct((3, 3, channels), F32),
        ),
        in_specs=[vmem] * 3,
        out_specs=(hbm,) * 4,
        scratch_shapes=[
            pltpu.VMEM((9, steps, channels), F32),
            pltpu.VMEM((1, channels), F32),
            pltpu.VMEM((3, 3, channels), F32),
            dma((12,)),
        ],
        name="finish",
    )(*[pltpu.with_memory_space_constraint(x, pltpu.VMEM) for x in held])
    return pred[None], one, bias[0], two


def solution(mesh):
    placed = (
        P("rep", "tile", None),
        P("rep", "tile", None),
        P("rep", "tile"),
        P("rep", "tile", None),
        P(),
        P(),
        P(),
        P(),
    )
    return jax.shard_map(
        functools.partial(on_device, mesh.shape["tile"], mesh.shape["rep"]),
        mesh=mesh,
        in_specs=placed,
        out_specs=(P("rep", "tile", None), P(), P(), P()),
        check_vma=False,
    )
```
